128 devices in a mesh: lat: 8 (over x, y_lo), lon: 16 (over y_hi, z, core).
Axes of the slice: x: 4, y: 4 (y_hi: 2, y_lo: 2; y = y_hi * 2 + y_lo), z: 4, core: 2. Of those that a mesh axis runs over, the one named last changes fastest.
Arguments:
- thermal_anomaly: float32 [25, 512, 2048], P(None, 'lat', 'lon'), may hold values from -6 to 6
- saltiness_anomaly: float32 [25, 512, 2048], P(None, 'lat', 'lon'), may hold values from -6 to 6
- zonal_transport_ratio: float32 [25, 512, 2048], P(None, 'lat', 'lon'), may hold values from -0.3 to 0.3
- meridional_transport_ratio: float32 [25, 512, 2048], P(None, 'lat', 'lon'), may hold values from -0.3 to 0.3
- zonal_density_tilt: float32 [25, 512, 2048], P(None, 'lat', 'lon'), may hold values from -0.5 to 0.5
- meridional_density_tilt: float32 [25, 512, 2048], P(None, 'lat', 'lon'), may hold values from -0.5 to 0.5
- diapycnal_diffusion_ratio: float32 [24, 512, 2048], P(None, 'lat', 'lon'), may hold values from 0.05 to 5
- ocean_depth_cells: int32 [512, 2048], P('lat', 'lon'), may hold values from 0 to 25
- partner_across_seam: int32 [2048], replicated, may hold values from 0 to 2047, as said below
Outputs:
- temperature_next: float32 [25, 512, 2048], P(None, 'lat', 'lon')
- salinity_next: float32 [25, 512, 2048], P(None, 'lat', 'lon')
The draws below stay inside these ranges and needn't reach their ends.
Inputs may be any that keep to these rules, and one draw needn't show every extreme that they name: partner_across_seam[i] = (2047 - i + s_i) mod 2048 with a per-column offset s_i of 0, 1 or 2 (a mirror about the grid's middle, displaced by up to two columns).
All inputs are finite; a program needn't handle non-finite values.
Results may differ from the reference program's by a relative error of at most 0.0003.
Values sent between devices are 32-bit elements; how exact they have to be, the bound alone decides.
A program may use at most 448 MiB of HBM per device.

```python
import math
import jax
import jax.numpy as jnp
from jax import lax

DEPTH_LAYERS = 25
MERIDIONAL_CELLS = 512
ZONAL_CELLS = 2048


def draw_partner_across_seam(key, part):
    column = jnp.arange(ZONAL_CELLS, dtype=jnp.int32)
    offsets = jax.random.randint(jax.random.fold_in(key, 7), (ZONAL_CELLS,), 0, 3).astype(jnp.int32)
    edge = (column == 0) | (column == ZONAL_CELLS - 1)
    offsets = jnp.where(edge, 0, offsets).astype(jnp.int32)
    return ((ZONAL_CELLS - 1 - column + offsets) % ZONAL_CELLS).astype(jnp.int32)


def plant(entries, stream_key, low, largest):
    index_at = [jax.random.randint(jax.random.fold_in(stream_key, axis), (), 0, length) for axis, length in enumerate(entries.shape)]
    main_axis = entries.shape.index(max(entries.shape))
    beside = index_at[:main_axis] + [(index_at[main_axis] + 1) % entries.shape[main_axis]] + index_at[main_axis + 1:]
    return entries.at[tuple(index_at)].set(low).at[tuple(beside)].set(largest)


def block_scale(stream_key, extent, pieces, least, top_value):
    factor_of, own = 1.0, jax.random.fold_in(stream_key, 6)
    for position, shards_of in pieces:
        steps = jnp.exp(jax.random.uniform(jax.random.fold_in(own, position), (shards_of,), jnp.float32, least / len(pieces), top_value / len(pieces)))
        factor_of = factor_of * jnp.repeat(steps, extent[position] // shards_of).reshape([-1 if axis == position else 1 for axis in range(len(extent))])
    return factor_of


def centred(stream_key, dims, deviation, bound, pieces=(), kind=jnp.bfloat16):
    entries = jax.random.normal(stream_key, dims, jnp.float32) * deviation
    if len(pieces) > 0:
        entries = block_scale(stream_key, dims, pieces, -0.22, 0.18) * entries
    return jnp.clip(entries, min=-bound, max=bound).astype(kind)


def setup_inputs(seed: int = 0) -> dict:
    keys = jax.random.split(jax.random.key(seed), 10)
    thermal_anomaly = centred(keys[0], (DEPTH_LAYERS, MERIDIONAL_CELLS, ZONAL_CELLS), 1.0, 6.0, ((1, 8), (2, 16)), jnp.float32)
    saltiness_anomaly = centred(keys[1], (DEPTH_LAYERS, MERIDIONAL_CELLS, ZONAL_CELLS), 1.0, 6.0, ((1, 8), (2, 16)), jnp.float32)
    zonal_transport_ratio = jnp.clip(jax.random.uniform(keys[2], (DEPTH_LAYERS, MERIDIONAL_CELLS, ZONAL_CELLS), jnp.float32, -0.3, 0.3) * block_scale(keys[2], (DEPTH_LAYERS, MERIDIONAL_CELLS, ZONAL_CELLS), ((1, 8), (2, 16)), -0.4, 0.0), -0.3, 0.3)
    meridional_transport_ratio = jnp.clip(jax.random.uniform(keys[3], (DEPTH_LAYERS, MERIDIONAL_CELLS, ZONAL_CELLS), jnp.float32, -0.3, 0.3) * block_scale(keys[3], (DEPTH_LAYERS, MERIDIONAL_CELLS, ZONAL_CELLS), ((1, 8), (2, 16)), -0.4, 0.0), -0.3, 0.3)
    zonal_density_tilt = jnp.clip(jax.random.uniform(keys[4], (DEPTH_LAYERS, MERIDIONAL_CELLS, ZONAL_CELLS), jnp.float32, -0.5, 0.5) * block_scale(keys[4], (DEPTH_LAYERS, MERIDIONAL_CELLS, ZONAL_CELLS), ((1, 8), (2, 16)), -0.4, 0.0), -0.5, 0.5)
    meridional_density_tilt = jnp.clip(jax.random.uniform(keys[5], (DEPTH_LAYERS, MERIDIONAL_CELLS, ZONAL_CELLS), jnp.float32, -0.5, 0.5) * block_scale(keys[5], (DEPTH_LAYERS, MERIDIONAL_CELLS, ZONAL_CELLS), ((1, 8), (2, 16)), -0.4, 0.0), -0.5, 0.5)
    diapycnal_diffusion_ratio = jnp.clip(jnp.exp(math.log(5.0) - 4.6051702 * jax.random.uniform(keys[6], (DEPTH_LAYERS - 1, MERIDIONAL_CELLS, ZONAL_CELLS), jnp.float32) ** block_scale(keys[6], (DEPTH_LAYERS - 1, MERIDIONAL_CELLS, ZONAL_CELLS), ((1, 8), (2, 16)), -0.2, 0.2)), 0.05, 5.0)
    ocean_depth_cells = plant(jax.random.randint(keys[7], (MERIDIONAL_CELLS, ZONAL_CELLS), 0, DEPTH_LAYERS + 1), jax.random.fold_in(keys[7], 1), 0, DEPTH_LAYERS).astype(jnp.int32)
    partner_across_seam = draw_partner_across_seam(jax.random.fold_in(keys[9], 71), 0)
    return {"thermal_anomaly": thermal_anomaly, "saltiness_anomaly": saltiness_anomaly, "zonal_transport_ratio": zonal_transport_ratio, "meridional_transport_ratio": meridional_transport_ratio, "zonal_density_tilt": zonal_density_tilt, "meridional_density_tilt": meridional_density_tilt, "diapycnal_diffusion_ratio": diapycnal_diffusion_ratio, "ocean_depth_cells": ocean_depth_cells, "partner_across_seam": partner_across_seam}


isopycnal_rate = 0.1


def advance(pad_tracer, pad_floor, pad_east, pad_north, pad_slope_east, pad_slope_north, diapycnal_diffusion_ratio):
    levels = pad_tracer.shape[1]
    meridional_extent = pad_tracer.shape[2] - 4
    zonal_extent = pad_tracer.shape[3] - 4
    level_index = lax.broadcasted_iota(jnp.int32, (levels, 1, 1), 0)
    wet_mask = (level_index < pad_floor[None]).astype(jnp.float32)
    masked = pad_tracer * wet_mask
    zero_layer = jnp.zeros_like(wet_mask[:1])
    above_cells = jnp.concatenate([masked[:, :1], masked[:, :-1]], 1)
    below_cells = jnp.concatenate([masked[:, 1:], masked[:, -1:]], 1)
    wet_above = jnp.concatenate([zero_layer, wet_mask[:-1]], 0)
    wet_below = jnp.concatenate([wet_mask[1:], zero_layer], 0)
    vertical = 0.5 * (jnp.where(wet_above > 0, above_cells, masked) - jnp.where(wet_below > 0, below_cells, masked))

    def window_of(values, shift_row, shift_col):
        return values[..., 2 + shift_row:2 + shift_row + meridional_extent, 2 + shift_col:2 + shift_col + zonal_extent]

    def face_flux(shift_row, shift_col, step_row, step_col, velocity_pad, slope_pad):
        behind = window_of(masked, shift_row - step_row, shift_col - step_col)
        centre = window_of(masked, shift_row, shift_col)
        ahead = window_of(masked, shift_row + step_row, shift_col + step_col)
        beyond = window_of(masked, shift_row + 2 * step_row, shift_col + 2 * step_col)
        open_face = window_of(wet_mask, shift_row, shift_col) * window_of(wet_mask, shift_row + step_row, shift_col + step_col)
        velocity = window_of(velocity_pad, shift_row, shift_col)
        upwind = jnp.where(velocity > 0, (5.0 * centre + 2.0 * ahead - behind) / 6.0, (2.0 * centre + 5.0 * ahead - beyond) / 6.0)
        carried = velocity * open_face * upwind
        slope_face = window_of(slope_pad, shift_row, shift_col)
        gradient = (ahead - centre) + slope_face * 0.5 * (window_of(vertical, shift_row, shift_col) + window_of(vertical, shift_row + step_row, shift_col + step_col))
        return carried, isopycnal_rate * open_face * gradient

    carried_east, diffused_east = face_flux(0, 0, 0, 1, pad_east, pad_slope_east)
    carried_west, diffused_west = face_flux(0, -1, 0, 1, pad_east, pad_slope_east)
    carried_north, diffused_north = face_flux(0, 0, 1, 0, pad_north, pad_slope_north)
    carried_south, diffused_south = face_flux(-1, 0, 1, 0, pad_north, pad_slope_north)
    interim = window_of(masked, 0, 0) - (carried_east - carried_west) - (carried_north - carried_south)
    interim = interim + (diffused_east - diffused_west) + (diffused_north - diffused_south)
    wet_core = window_of(wet_mask, 0, 0)
    coupling = diapycnal_diffusion_ratio * wet_core[:-1] * wet_core[1:]
    ratios = []
    sweeps = []
    for layer in range(levels):
        above_rate = coupling[layer - 1] if layer > 0 else 0.0
        below_rate = coupling[layer] if layer < levels - 1 else 0.0
        pivot_value = 1.0 + above_rate + below_rate
        source = interim[:, layer]
        if layer > 0:
            pivot_value = pivot_value + above_rate * ratios[-1]
            source = source + above_rate * sweeps[-1]
        ratios.append(-below_rate / pivot_value)
        sweeps.append(source / pivot_value)
    solved = [sweeps[-1]]
    for layer in range(levels - 2, -1, -1):
        solved.insert(0, sweeps[layer] - ratios[layer] * solved[0])
    return jnp.stack(solved, 1) * wet_core


def extend_field(values, partner_across_seam):
    total_rows = values.shape[-2]
    ghost = jnp.take(values[..., total_rows - 2:total_rows, :][..., ::-1, :], partner_across_seam, axis=-1)
    southern = jnp.zeros_like(values[..., :2, :])
    tall = jnp.concatenate([southern, values, ghost], -2)
    return jnp.concatenate([tall[..., -2:], tall, tall[..., :2]], -1)


def reference(thermal_anomaly, saltiness_anomaly, zonal_transport_ratio, meridional_transport_ratio, zonal_density_tilt, meridional_density_tilt, diapycnal_diffusion_ratio, ocean_depth_cells, partner_across_seam):
    pad_floor = extend_field(ocean_depth_cells, partner_across_seam)
    pad_east = extend_field(zonal_transport_ratio, partner_across_seam)
    pad_north = extend_field(meridional_transport_ratio, partner_across_seam)
    pad_slope_east = extend_field(zonal_density_tilt, partner_across_seam)
    pad_slope_north = extend_field(meridional_density_tilt, partner_across_seam)
    results = []
    for scalar_quantity in (thermal_anomaly, saltiness_anomaly):
        pad_tracer = extend_field(scalar_quantity, partner_across_seam)[None]
        results.append(advance(pad_tracer, pad_floor, pad_east, pad_north, pad_slope_east, pad_slope_north, diapycnal_diffusion_ratio)[0])
    return (results[0], results[1])
```

```python
import functools

import jax
import jax.numpy as jnp
from jax import lax
from jax.experimental import pallas as pl
from jax.experimental.pallas import tpu as pltpu
from jax.sharding import PartitionSpec as P

isopycnal_rate = 0.1
MESH = pl.DeviceIdType.MESH
f32 = jnp.float32
OFF = 8


def along_lanes(x, shift):
    return pltpu.roll(x, shift % 128, 1)


def along_rows(x, shift):
    return pltpu.roll(x, shift % 8, 0)


def row_of(ref, *index):
    *lead, row = index
    return jnp.broadcast_to(ref[(*lead, pl.ds(row, 1), slice(None))], (8, 128))


def edge_terms(place, turn, level, near, beyond, near_floor, beyond_floor, near_vertical, beyond_vertical, speed, slope):
    high = place >= 2
    own_floor = jnp.where(high, beyond_floor, near_floor)
    behind = turn(near, 1)
    ahead = turn(beyond, 1)
    weight = jnp.abs(speed) * (1.0 / 6.0)
    full = 0.5 * speed * (near + ahead) - (weight + isopycnal_rate) * (ahead - near)
    full = full + weight * jnp.where(speed > 0, near - behind, beyond - ahead)
    full = full - (0.25 * isopycnal_rate) * slope * (near_vertical + turn(beyond_vertical, 1))
    full = jnp.where(level < jnp.minimum(near_floor, turn(beyond_floor, 1)), full, 0.0)
    part = weight * (beyond - turn(near, -1))
    part = jnp.where(jnp.where(high, speed, -speed) > 0, part, 0.0)
    part = jnp.where(level < jnp.minimum(own_floor, turn(own_floor, -1)), part, 0.0)
    flux = jnp.where((place & 1) == 1, full, part)
    at_west = jnp.where(place == 2, turn(flux, -1), jnp.where(place == 0, 0.0, turn(flux, 1)))
    return at_west - jnp.where(place == 3, 0.0, flux)


def step_kernel(
    axes,
    temp_hbm,
    salt_hbm,
    east_hbm,
    north_hbm,
    tilt_east_hbm,
    tilt_north_hbm,
    mix_hbm,
    floor_hbm,
    partner_hbm,
    temp_out,
    salt_out,
    raw,
    mix,
    floor,
    partner,
    cells,
    vertical,
    flux_north,
    interim,
    pivot,
    lower,
    upper,
    floor_east,
    floor_north,
    packed,
    fix,
    east_message,
    west_message,
    north_message,
    south_message,
    from_west,
    from_east,
    from_south,
    from_north,
    from_seam,
    load_sem,
    store_sem,
    send_sem,
    recv_sem,
):
    lats, lons = axes
    levels, rows, _ = mix.shape[0] + 1, mix.shape[1], mix.shape[2]
    tiles = rows // 8
    lat, lon = lax.axis_index("lat"), lax.axis_index("lon")
    at_south, at_north = lat == 0, lat == lats - 1
    east, west = lax.rem(lon + 1, lons), lax.rem(lon + lons - 1, lons)
    facing, beside = lons - 1 - lon, lax.rem(lons - lon, lons)
    other = beside != lon

    def load(source, target, index):
        copy = pltpu.make_async_copy(source, target, load_sem.at[index])
        copy.start()
        return copy

    loads = [load(floor_hbm, floor.at[pl.ds(0, rows)], 0)]
    for i, ref in enumerate((temp_hbm, salt_hbm, east_hbm, tilt_east_hbm, north_hbm, tilt_north_hbm)):
        loads.append(load(ref, raw.at[i], 1 + i))
    loads.append(load(mix_hbm, mix, 7))
    loads.append(load(partner_hbm, partner, 8))

    barrier = pltpu.get_barrier_semaphore()

    def greet(target_lat, target_lon):
        pl.semaphore_signal(barrier, inc=1, device_id={"lat": target_lat, "lon": target_lon}, device_id_type=MESH)

    greet(lat, east)
    greet(lat, west)

    @pl.when(jnp.logical_not(at_south))
    def _():
        greet(lat - 1, lon)

    @pl.when(jnp.logical_not(at_north))
    def _():
        greet(lat + 1, lon)

    @pl.when(at_north)
    def _():
        greet(lat, facing)

    @pl.when(jnp.logical_and(at_north, other))
    def _():
        greet(lat, beside)

    def send(source, target, index, target_lat, target_lon, receive):
        return pltpu.make_async_remote_copy(
            src_ref=source,
            dst_ref=target,
            send_sem=send_sem.at[index],
            recv_sem=recv_sem.at[receive],
            device_id={"lat": target_lat, "lon": target_lon},
            device_id_type=MESH,
        )

    rows_only = north_message.at[pl.ds(0, south_message.shape[0])]
    to_east = send(east_message, from_west, 0, lat, east, 0)
    to_west = send(west_message, from_east, 1, lat, west, 1)
    to_north = send(north_message, from_south, 2, lat + 1, lon, 2)
    to_south = send(south_message, from_north, 3, lat - 1, lon, 3)
    to_facing = send(rows_only, from_north, 4, lat, facing, 3)
    to_beside = send(rows_only, from_seam, 5, lat, beside, 4)

    lane = lax.broadcasted_iota(jnp.int32, (8, 128), 1)
    sub = lax.broadcasted_iota(jnp.int32, (8, 128), 0)
    lane_place, lane_level = lane & 3, lane >> 2
    sub_place = sub & 3
    floor_lanes = (lane >> 1) == 52
    zero = jnp.zeros((8, 128), f32)

    for copy in loads[:5]:
        copy.wait()

    @pl.loop(0, tiles)
    def _(t):
        at = pl.multiple_of(8 * t, 8)
        here, padded = pl.ds(at, 8), pl.ds(at + OFF, 8)
        depth = floor[here]
        packs = [zero, zero, zero, zero]
        before, now = [None, None], [None, None]
        for k in range(levels + 1):
            if k < levels:
                wet = depth > k
                taken = lane_level == k
                values = [jnp.where(wet, raw[q, k, here], 0.0) for q in range(2)]
                values += [raw[q, k, here] for q in (2, 3)]
                for q in range(4):
                    packs[q] = jnp.where(taken, along_lanes(values[q], 4 * k + 2), packs[q])
                for q in range(2):
                    cells[q, k, padded] = values[q]
            for q in range(2):
                if k > 0:
                    below = jnp.where(wet, values[q], now[q]) if k < levels else now[q]
                    vertical[q, k - 1, padded] = (before[q] if k > 1 else now[q]) - below
                before[q], now[q] = now[q], values[q]
        for q in range(4):
            packed[q, here] = packs[q]
        depth_f = depth.astype(f32)
        high = lane_place >= 2
        east_message[0, here] = jnp.where(high, along_lanes(packs[0], 2), packs[1])
        speeds = jnp.where(lane_place == 3, along_lanes(packs[2], 2), along_lanes(packs[3], 1))
        east_message[1, here] = jnp.where(floor_lanes, along_lanes(depth_f, 104 - 126), speeds)
        tracers = jnp.where(high, packs[1], along_lanes(packs[0], -2))
        west_message[here] = jnp.where(floor_lanes, along_lanes(depth_f, 104), tracers)
        floor_east[here] = jnp.where(lane == 127, 0, jnp.minimum(depth, along_lanes(depth, -1)))

    for copy in loads[5:7]:
        copy.wait()
    last = levels // 2
    north_message[last] = zero
    south_message[last] = zero
    north_message[north_message.shape[0] - 1] = zero
    top, bottom = pl.ds(rows - 2, 2), pl.ds(0, 2)
    for k in range(levels):
        m, odd = k // 2, k % 2
        for q in range(2):
            north_message[m, pl.ds(4 * q + 2 - 2 * odd, 2)] = cells[q, k, pl.ds(OFF + rows - 2, 2)]
            south_message[m, pl.ds(4 * q + 2 * odd, 2)] = cells[q, k, pl.ds(OFF, 2)]
            north_message[last + 1 + k // 4, pl.ds(2 * (k % 4) + q, 1)] = raw[4 + q, k, pl.ds(rows - 1, 1)]
    north_message[last, pl.ds(0, 2)] = floor[top].astype(f32)
    south_message[last, pl.ds(2, 2)] = floor[bottom].astype(f32)
    for t in range(tiles):
        both = jnp.minimum(floor[pl.ds(8 * t, 8)], floor[pl.ds(8 * t + 1, 8)])
        floor_north[pl.ds(8 * t, 8)] = both if t < tiles - 1 else jnp.where(sub == 7, 0, both)

    pl.semaphore_wait(barrier, jnp.where(at_south, 3, jnp.where(jnp.logical_and(at_north, other), 5, 4)))

    to_east.start()
    to_west.start()

    @pl.when(jnp.logical_not(at_south))
    def _():
        to_south.start()

    @pl.when(jnp.logical_not(at_north))
    def _():
        to_north.start()

    @pl.when(at_north)
    def _():
        to_facing.start()

    @pl.when(jnp.logical_and(at_north, other))
    def _():
        to_beside.start()

    for copy in loads[7:]:
        copy.wait()

    for q in range(2):
        flux_north[q, pl.ds(0, OFF)] = zero

    def main(k, carry):
        above_rates, above_factors = carry
        next_rates, next_factors = [], []
        for t in range(tiles):
            here = pl.ds(8 * t, 8)
            depth = floor[here]
            open_east, open_north = floor_east[here] > k, floor_north[here] > k
            speed_east, speed_north = raw[2, k, here], raw[4, k, here]
            weight_east, weight_north = jnp.abs(speed_east) * (1.0 / 6.0), jnp.abs(speed_north) * (1.0 / 6.0)
            spread_east, spread_north = weight_east + isopycnal_rate, weight_north + isopycnal_rate
            half_east, half_north = 0.5 * speed_east, 0.5 * speed_north
            forth_east, forth_north = speed_east > 0, speed_north > 0
            tilt_east, tilt_north = (0.25 * isopycnal_rate) * raw[3, k, here], (0.25 * isopycnal_rate) * raw[5, k, here]
            for q in range(2):
                row = OFF + 8 * t
                centre = cells[q, k, pl.ds(row, 8)]
                slant = vertical[q, k, pl.ds(row, 8)]
                ahead, beyond = cells[q, k, pl.ds(row + 1, 8)], cells[q, k, pl.ds(row + 2, 8)]
                rise, rise_behind, rise_ahead = ahead - centre, centre - cells[q, k, pl.ds(row - 1, 8)], beyond - ahead
                if t == 0:
                    rise_behind = jnp.where(sub == 0, 0.0, rise_behind)
                if t == tiles - 1:
                    rise_ahead = jnp.where(sub >= 6, 0.0, rise_ahead)
                flux = half_north * (centre + ahead) - spread_north * rise
                flux = flux + weight_north * jnp.where(forth_north, rise_behind, rise_ahead)
                flux = flux - tilt_north * (slant + vertical[q, k, pl.ds(row + 1, 8)])
                flux = jnp.where(open_north, flux, 0.0)
                flux_north[q, pl.ds(row, 8)] = flux
                result = centre - flux + flux_north[q, pl.ds(row - 1, 8)]
                ahead = along_lanes(centre, -1)
                rise = jnp.where(lane == 127, 0.0, ahead - centre)
                flux = half_east * (centre + ahead) - spread_east * rise
                flux = flux + weight_east * jnp.where(forth_east, along_lanes(rise, 1), along_lanes(rise, -1))
                flux = flux - tilt_east * (slant + along_lanes(slant, -1))
                flux = jnp.where(open_east, flux, 0.0)
                interim[q, k, here] = result - flux + along_lanes(flux, 1)
            above = above_rates[t]
            below = jnp.where(depth > k + 1, mix[jnp.minimum(k, levels - 2), here], 0.0)
            inverse = 1.0 / (1.0 + above + below - above * above_factors[t])
            pivot[k, here] = inverse
            lower[k, here] = above * inverse
            factor = below * inverse
            upper[k, here] = factor
            next_rates.append(below)
            next_factors.append(factor)
        return tuple(next_rates), tuple(next_factors)

    lax.fori_loop(0, levels, main, ((zero,) * tiles, (zero,) * tiles))

    to_east.wait()
    to_west.wait()

    def lane_vertical(values, depth):
        above = jnp.where(lane_level == 0, values, along_lanes(values, 4))
        return above - jnp.where(level_f + 1.0 < depth, along_lanes(values, -4), values)

    level_f = lane_level.astype(f32)

    @pl.loop(0, tiles)
    def _(t):
        here = pl.ds(pl.multiple_of(8 * t, 8), 8)
        depth = floor[here].astype(f32)
        tracers_west, speeds_west, tracers_east = from_west[0, here], from_west[1, here], from_east[here]

        def column(values, index):
            return jnp.broadcast_to(values[:, index : index + 1], (8, 128))

        def of_four(a, b, c, d):
            return jnp.where(lane_place < 2, jnp.where(lane_place == 0, a, b), jnp.where(lane_place == 2, c, d))

        own_floor = of_four(column(depth, 126), column(depth, 127), column(depth, 0), column(depth, 1))
        far_floor = of_four(
            column(tracers_east, 104), column(tracers_east, 105), column(speeds_west, 104), column(speeds_west, 105)
        )
        speed = jnp.where(lane_place == 3, speeds_west, packed[2, here])
        slope = jnp.where(lane_place == 3, along_lanes(speeds_west, 1), packed[3, here])
        high = lane_place >= 2
        far = (
            jnp.where(high, tracers_west, tracers_east),
            jnp.where(high, along_lanes(tracers_west, 2), along_lanes(tracers_east, -2)),
        )
        near_floor, beyond_floor = jnp.where(high, far_floor, own_floor), jnp.where(high, own_floor, far_floor)
        for q in range(2):
            own = packed[q, here]
            near, beyond = jnp.where(high, far[q], own), jnp.where(high, own, far[q])
            fix[q, here] = edge_terms(
                lane_place,
                along_lanes,
                level_f,
                near,
                beyond,
                near_floor,
                beyond_floor,
                lane_vertical(near, near_floor),
                lane_vertical(beyond, beyond_floor),
                speed,
                slope,
            )

    @pl.when(at_south)
    def _():
        from_south[...] = jnp.zeros(from_south.shape, f32)

    @pl.when(jnp.logical_not(at_south))
    def _():
        to_south.wait_send()
        to_north.wait_recv()

    @pl.when(jnp.logical_not(at_north))
    def _():
        to_north.wait_send()
        to_south.wait_recv()

    @pl.when(at_north)
    def _():
        to_facing.wait()

    @pl.when(jnp.logical_and(at_north, other))
    def _():
        to_beside.wait()

    @pl.when(jnp.logical_and(at_north, jnp.logical_not(other)))
    def _():
        from_seam[...] = rows_only[...]

    @pl.when(at_north)
    def _():
        column = row_of(partner, lon)
        index = (column - 128 * facing + 128 * lons) & (128 * lons - 1)
        inside = index < 128
        index = index & 127
        for m in range(from_north.shape[0]):
            facing_rows = jnp.take_along_axis(from_north[m], index, axis=1, mode="promise_in_bounds")
            beside_rows = jnp.take_along_axis(from_seam[m], index, axis=1, mode="promise_in_bounds")
            found = jnp.where(inside, facing_rows, beside_rows)
            from_north[m] = jnp.where(
                sub_place < 2,
                jnp.where(sub_place == 0, along_rows(found, -3), along_rows(found, -1)),
                jnp.where(sub_place == 2, along_rows(found, 1), along_rows(found, 3)),
            )

    def of_rows(a, b, c, d):
        return jnp.where(sub_place < 2, jnp.where(sub_place == 0, a, b), jnp.where(sub_place == 2, c, d))

    own_floor = of_rows(row_of(floor, rows - 2), row_of(floor, rows - 1), row_of(floor, 0), row_of(floor, 1)).astype(f32)
    far_floor = of_rows(
        row_of(from_north, last, 2), row_of(from_north, last, 3), row_of(from_south, last, 0), row_of(from_south, last, 1)
    )
    high = sub_place >= 2

    def own_rows(k):
        lo = jnp.where(sub < 2, cells[0, k, pl.ds(OFF + rows - 2, 8)], cells[0, k, pl.ds(OFF - 2, 8)])
        hi = jnp.where(sub < 6, cells[1, k, pl.ds(OFF + rows - 6, 8)], cells[1, k, pl.ds(OFF - 6, 8)])
        return jnp.where(sub < 4, lo, hi)

    def far_rows(k):
        south, north = from_south[k // 2], from_north[k // 2]
        if k % 2 == 1:
            south, north = along_rows(south, 2), along_rows(north, -2)
        return jnp.where(high, south, north)

    near_floor, beyond_floor = jnp.where(high, far_floor, own_floor), jnp.where(high, own_floor, far_floor)
    near, beyond = [], []

    def row_vertical(column, depth, k):
        above = column[max(k - 1, 0)]
        below = jnp.where(depth > k + 1.0, column[k + 1], column[k]) if k + 1 < levels else column[k]
        return above - below

    for k in range(levels):
        while len(near) < min(k + 2, levels):
            own, far = own_rows(len(near)), far_rows(len(near))
            near.append(jnp.where(high, far, own))
            beyond.append(jnp.where(high, own, far))
        speed = of_rows(
            row_of(raw, 4, k, rows - 2),
            row_of(raw, 4, k, rows - 1),
            row_of(raw, 4, k, 0),
            row_of(from_south, last + 1 + k // 4, 2 * (k % 4)),
        )
        slope = jnp.where(high, row_of(from_south, last + 1 + k // 4, 2 * (k % 4) + 1), row_of(raw, 5, k, rows - 1))
        terms = edge_terms(
            sub_place,
            along_rows,
            float(k),
            near[k],
            beyond[k],
            near_floor,
            beyond_floor,
            row_vertical(near, near_floor, k),
            row_vertical(beyond, beyond_floor, k),
            speed,
            slope,
        )
        for q in range(2):
            turned = along_rows(terms, 2 if q else -2)
            first, final = pl.ds(0, 8), pl.ds(rows - 8, 8)
            interim[q, k, first] = interim[q, k, first] + jnp.where(sub < 2, turned, 0.0)
            interim[q, k, final] = interim[q, k, final] + jnp.where(sub >= 6, turned, 0.0)

    edge = ((lane + 2) & 127) < 4

    def down(k, carry):
        new = []
        for t in range(tiles):
            here = pl.ds(8 * t, 8)
            inverse, factor = pivot[k, here], lower[k, here]
            for q in range(2):
                shift = lax.rem(126 + 128 - 4 * k, 128)
                source = interim[q, k, here] + jnp.where(edge, pltpu.roll(fix[q, here], shift, 1), 0.0)
                value = source * inverse + factor * carry[2 * t + q]
                interim[q, k, here] = value
                new.append(value)
        return tuple(new)

    lax.fori_loop(0, levels, down, (zero,) * (2 * tiles))

    def up(step, carry):
        k = levels - 1 - step
        new = []
        for t in range(tiles):
            here = pl.ds(8 * t, 8)
            factor, wet = upper[k, here], floor[here] > k
            for q in range(2):
                value = interim[q, k, here] + factor * carry[2 * t + q]
                interim[q, k, here] = jnp.where(wet, value, 0.0)
                new.append(value)
        return tuple(new)

    state = (zero,) * (2 * tiles)
    part = 5
    stores = []
    for step in range(0, levels, part):
        state = lax.fori_loop(step, step + part, up, state)
        done = pl.ds(levels - step - part, part)
        for q, target in enumerate((temp_out, salt_out)):
            copy = pltpu.make_async_copy(interim.at[q, done], target.at[done], store_sem.at[len(stores)])
            copy.start()
            stores.append(copy)
    for copy in stores:
        copy.wait()


def local(axes, *arguments):
    levels, rows, columns = arguments[0].shape
    partner = arguments[8].reshape(-1, columns)
    shape = (levels, rows, columns)
    padded = (2, levels, rows + 2 * OFF, columns)
    pairs = levels // 2 + 1
    north_tiles = pairs + (levels + 3) // 4
    out = jax.ShapeDtypeStruct(shape, f32)
    return pl.pallas_call(
        functools.partial(step_kernel, axes),
        out_shape=(out, out),
        in_specs=[pl.BlockSpec(memory_space=pltpu.HBM)] * 9,
        out_specs=[pl.BlockSpec(memory_space=pl.ANY)] * 2,
        scratch_shapes=[
            pltpu.VMEM((6, *shape), f32),
            pltpu.VMEM((levels - 1, rows, columns), f32),
            pltpu.VMEM((rows + OFF, columns), jnp.int32),
            pltpu.VMEM(partner.shape, jnp.int32),
            pltpu.VMEM(padded, f32),
            pltpu.VMEM(padded, f32),
            pltpu.VMEM((2, rows + OFF, columns), f32),
            pltpu.VMEM((2, *shape), f32),
            pltpu.VMEM(shape, f32),
            pltpu.VMEM(shape, f32),
            pltpu.VMEM(shape, f32),
            pltpu.VMEM((rows, columns), jnp.int32),
            pltpu.VMEM((rows, columns), jnp.int32),
            pltpu.VMEM((4, rows, columns), f32),
            pltpu.VMEM((2, rows, columns), f32),
            pltpu.VMEM((2, rows, columns), f32),
            pltpu.VMEM((rows, columns), f32),
            pltpu.VMEM((north_tiles, 8, columns), f32),
            pltpu.VMEM((pairs, 8, columns), f32),
            pltpu.VMEM((2, rows, columns), f32),
            pltpu.VMEM((rows, columns), f32),
            pltpu.VMEM((north_tiles, 8, columns), f32),
            pltpu.VMEM((pairs, 8, columns), f32),
            pltpu.VMEM((pairs, 8, columns), f32),
            pltpu.SemaphoreType.DMA((9,)),
            pltpu.SemaphoreType.DMA((10,)),
            pltpu.SemaphoreType.DMA((6,)),
            pltpu.SemaphoreType.DMA((5,)),
        ],
        compiler_params=pltpu.CompilerParams(
            collective_id=0, has_side_effects=True, vmem_limit_bytes=40 * 2**20
        ),
        name="tracer_step",
    )(*[pltpu.with_memory_space_constraint(a, pltpu.HBM) for a in (*arguments[:8], partner)])


def solution(mesh):
    axes = (mesh.shape["lat"], mesh.shape["lon"])
    block = P(None, "lat", "lon")
    return jax.shard_map(
        functools.partial(local, axes),
        mesh=mesh,
        in_specs=(block,) * 7 + (P("lat", "lon"), P()),
        out_specs=(block, block),
        check_vma=False,
    )
```

```python
import functools

import jax
import jax.numpy as jnp
from jax import lax
from jax.experimental import pallas as pl
from jax.experimental.pallas import tpu as pltpu
from jax.sharding import PartitionSpec as P

isopycnal_rate = 0.1
MESH = pl.DeviceIdType.MESH
f32 = jnp.float32
OFF = 8


def along_lanes(x, shift):
    return pltpu.roll(x, shift % 128, 1)


def along_rows(x, shift):
    return pltpu.roll(x, shift % 8, 0)


def row_of(ref, *index):
    *lead, row = index
    return jnp.broadcast_to(ref[(*lead, pl.ds(row, 1), slice(None))], (8, 128))


def edge_terms(place, turn, level, near, beyond, near_floor, beyond_floor, near_vertical, beyond_vertical, speed, slope):
    high = place >= 2
    own_floor = jnp.where(high, beyond_floor, near_floor)
    behind = turn(near, 1)
    ahead = turn(beyond, 1)
    weight = jnp.abs(speed) * (1.0 / 6.0)
    full = 0.5 * speed * (near + ahead) - (weight + isopycnal_rate) * (ahead - near)
    full = full + weight * jnp.where(speed > 0, near - behind, beyond - ahead)
    full = full - (0.25 * isopycnal_rate) * slope * (near_vertical + turn(beyond_vertical, 1))
    full = jnp.where(level < jnp.minimum(near_floor, turn(beyond_floor, 1)), full, 0.0)
    part = weight * (beyond - turn(near, -1))
    part = jnp.where(jnp.where(high, speed, -speed) > 0, part, 0.0)
    part = jnp.where(level < jnp.minimum(own_floor, turn(own_floor, -1)), part, 0.0)
    flux = jnp.where((place & 1) == 1, full, part)
    at_west = jnp.where(place == 2, turn(flux, -1), jnp.where(place == 0, 0.0, turn(flux, 1)))
    return at_west - jnp.where(place == 3, 0.0, flux)


def step_kernel(
    axes,
    temp_hbm,
    salt_hbm,
    east_hbm,
    north_hbm,
    tilt_east_hbm,
    tilt_north_hbm,
    mix_hbm,
    floor_hbm,
    partner_hbm,
    solved,
    fix_columns,
    fix_rows,
    raw,
    mix,
    floor,
    partner,
    cells,
    vertical,
    flux_north,
    sweep,
    pivot,
    rate,
    upper,
    floor_east,
    floor_north,
    packed,
    scan,
    row_factors,
    east_message,
    west_message,
    north_message,
    south_message,
    beside_message,
    from_west,
    from_east,
    from_south,
    from_north,
    from_beside,
    load_sem,
    send_sem,
    recv_sem,
):
    lats, lons = axes
    levels, rows = mix.shape[0] + 1, mix.shape[1]
    tiles = rows // 8
    lat, lon = lax.axis_index("lat"), lax.axis_index("lon")
    at_south, at_north = lat == 0, lat == lats - 1
    east, west = lax.rem(lon + 1, lons), lax.rem(lon + lons - 1, lons)
    facing, beside = lons - 1 - lon, lax.rem(lons - lon, lons)
    other = beside != lon
    parts = 4 if tiles % 4 == 0 else 1
    part_rows = rows // parts

    barrier = pltpu.get_barrier_semaphore()

    def greet(target_lat, target_lon):
        pl.semaphore_signal(barrier, inc=1, device_id={"lat": target_lat, "lon": target_lon}, device_id_type=MESH)

    greet(lat, east)
    greet(lat, west)

    @pl.when(jnp.logical_not(at_south))
    def _():
        greet(lat - 1, lon)

    @pl.when(jnp.logical_not(at_north))
    def _():
        greet(lat + 1, lon)

    @pl.when(at_north)
    def _():
        greet(lat, facing)

    @pl.when(jnp.logical_and(at_north, other))
    def _():
        greet(lat, beside)

    def load(source, target, index):
        copy = pltpu.make_async_copy(source, target, load_sem.at[index])
        copy.start()
        return copy

    first_loads = [load(floor_hbm, floor.at[pl.ds(0, rows)], 0)]
    part_loads = []
    for p in range(parts):
        chunk = pl.ds(p * part_rows, part_rows)
        part_loads.append(
            [
                load(ref.at[:, chunk], raw.at[i, :, chunk], 4 + 4 * p + i)
                for i, ref in enumerate((temp_hbm, salt_hbm, east_hbm, tilt_east_hbm))
            ]
        )
    north_loads = [load(north_hbm, raw.at[4], 20), load(tilt_north_hbm, raw.at[5], 21)]
    last_loads = [load(mix_hbm, mix, 22), load(partner_hbm, partner, 23)]

    def send(source, target, index, target_lat, target_lon, receive):
        return pltpu.make_async_remote_copy(
            src_ref=source,
            dst_ref=target,
            send_sem=send_sem.at[index],
            recv_sem=recv_sem.at[receive],
            device_id={"lat": target_lat, "lon": target_lon},
            device_id_type=MESH,
        )

    rows_only = north_message.at[pl.ds(0, south_message.shape[0])]
    to_east = send(east_message, from_west, 0, lat, east, 0)
    to_west = send(west_message, from_east, 1, lat, west, 1)
    to_north = send(north_message, from_south, 2, lat + 1, lon, 2)
    to_south = send(south_message, from_north, 3, lat - 1, lon, 3)
    to_facing = send(rows_only, from_north, 4, lat, facing, 3)
    to_beside = send(beside_message, from_beside, 5, lat, beside, 4)

    lane = lax.broadcasted_iota(jnp.int32, (8, 128), 1)
    sub = lax.broadcasted_iota(jnp.int32, (8, 128), 0)
    lane_place, lane_level = lane & 3, lane >> 2
    level_f = lane_level.astype(f32)
    sub_place = sub & 3
    floor_lanes = (lane >> 1) == 52
    zero = jnp.zeros((8, 128), f32)

    def column(values, index):
        return jnp.broadcast_to(values[:, index : index + 1], (8, 128))

    def of_four(a, b, c, d):
        return jnp.where(lane_place < 2, jnp.where(lane_place == 0, a, b), jnp.where(lane_place == 2, c, d))

    def of_rows(a, b, c, d):
        return jnp.where(sub_place < 2, jnp.where(sub_place == 0, a, b), jnp.where(sub_place == 2, c, d))

    def prepare(at):
        here, padded = pl.ds(at, 8), pl.ds(at + OFF, 8)
        depth = floor[here]
        packs = [zero, zero, zero, zero]
        before, now = [None, None], [None, None]
        for k in range(levels + 1):
            if k < levels:
                wet = depth > k
                taken = lane_level == k
                values = [jnp.where(wet, raw[q, k, here], 0.0) for q in range(2)]
                values += [raw[q, k, here] for q in (2, 3)]
                for q in range(4):
                    packs[q] = jnp.where(taken, along_lanes(values[q], 4 * k + 2), packs[q])
                for q in range(2):
                    cells[q, k, padded] = values[q]
            for q in range(2):
                if k > 0:
                    below = jnp.where(wet, values[q], now[q]) if k < levels else now[q]
                    vertical[q, k - 1, padded] = (before[q] if k > 1 else now[q]) - below
                before[q], now[q] = now[q], values[q]
        depth_f = depth.astype(f32)
        own_floor = of_four(column(depth_f, 126), column(depth_f, 127), column(depth_f, 0), column(depth_f, 1))
        for q in range(4):
            packed[q, here] = packs[q]
        packed[4, here] = own_floor
        high = lane_place >= 2
        east_message[0, here] = jnp.where(high, along_lanes(packs[0], 2), packs[1])
        speeds = jnp.where(lane_place == 3, along_lanes(packs[2], 2), along_lanes(packs[3], 1))
        east_message[1, here] = jnp.where(high, speeds, own_floor)
        tracers = jnp.where(high, packs[1], along_lanes(packs[0], -2))
        west_message[here] = jnp.where(floor_lanes, along_lanes(depth_f, 104), tracers)
        floor_east[here] = jnp.where(lane == 127, 0, jnp.minimum(depth, along_lanes(depth, -1)))

    for copy in first_loads:
        copy.wait()
    for p in range(parts):
        for copy in part_loads[p]:
            copy.wait()

        @pl.loop(0, part_rows // 8)
        def _(t, p=p):
            prepare(pl.multiple_of(p * part_rows + 8 * t, 8))

    pl.semaphore_wait(barrier, jnp.where(at_south, 3, jnp.where(jnp.logical_and(at_north, other), 5, 4)))
    to_east.start()
    to_west.start()

    for copy in north_loads:
        copy.wait()
    last = levels // 2
    north_message[last] = zero
    south_message[last] = zero
    north_message[north_message.shape[0] - 1] = zero
    top, bottom = pl.ds(rows - 2, 2), pl.ds(0, 2)
    for k in range(levels):
        m, odd = k // 2, k % 2
        for q in range(2):
            north_message[m, pl.ds(4 * q + 2 - 2 * odd, 2)] = cells[q, k, pl.ds(OFF + rows - 2, 2)]
            south_message[m, pl.ds(4 * q + 2 * odd, 2)] = cells[q, k, pl.ds(OFF, 2)]
            north_message[last + 1 + k // 4, pl.ds(2 * (k % 4) + q, 1)] = raw[4 + q, k, pl.ds(rows - 1, 1)]
    north_message[last, pl.ds(0, 2)] = floor[top].astype(f32)
    south_message[last, pl.ds(2, 2)] = floor[bottom].astype(f32)

    @pl.when(at_north)
    def _():
        pack = zero
        for m in range(last + 1):
            pack = jnp.where((lane >> 1) == m, along_lanes(north_message[m], 2 * m), pack)
        beside_message[...] = pack
        to_facing.start()

    @pl.when(jnp.logical_and(at_north, other))
    def _():
        to_beside.start()

    @pl.when(jnp.logical_not(at_south))
    def _():
        to_south.start()

    @pl.when(jnp.logical_not(at_north))
    def _():
        to_north.start()

    for t in range(tiles):
        both = jnp.minimum(floor[pl.ds(8 * t, 8)], floor[pl.ds(8 * t + 1, 8)])
        floor_north[pl.ds(8 * t, 8)] = both if t < tiles - 1 else jnp.where(sub == 7, 0, both)

    for copy in last_loads:
        copy.wait()

    for q in range(2):
        flux_north[q, pl.ds(0, OFF)] = zero

    def main(k, state):
        for t in range(tiles):
            here = pl.ds(8 * t, 8)
            depth = floor[here]
            open_east, open_north = floor_east[here] > k, floor_north[here] > k
            speed_east, speed_north = raw[2, k, here], raw[4, k, here]
            weight_east, weight_north = jnp.abs(speed_east) * (1.0 / 6.0), jnp.abs(speed_north) * (1.0 / 6.0)
            spread_east, spread_north = weight_east + isopycnal_rate, weight_north + isopycnal_rate
            half_east, half_north = 0.5 * speed_east, 0.5 * speed_north
            forth_east, forth_north = speed_east > 0, speed_north > 0
            tilt_east, tilt_north = (0.25 * isopycnal_rate) * raw[3, k, here], (0.25 * isopycnal_rate) * raw[5, k, here]
            above, above_factor, *values = state[t]
            below = jnp.where(depth > k + 1, mix[jnp.minimum(k, levels - 2), here], 0.0)
            inverse = 1.0 / (1.0 + above + below - above * above_factor)
            factor = below * inverse
            pivot[k, here] = inverse
            rate[k, here] = below
            upper[k, here] = factor
            for q in range(2):
                row = OFF + 8 * t
                centre = cells[q, k, pl.ds(row, 8)]
                slant = vertical[q, k, pl.ds(row, 8)]
                ahead, beyond = cells[q, k, pl.ds(row + 1, 8)], cells[q, k, pl.ds(row + 2, 8)]
                rise, rise_behind, rise_ahead = ahead - centre, centre - cells[q, k, pl.ds(row - 1, 8)], beyond - ahead
                if t == 0:
                    rise_behind = jnp.where(sub == 0, 0.0, rise_behind)
                if t == tiles - 1:
                    rise_ahead = jnp.where(sub >= 6, 0.0, rise_ahead)
                flux = half_north * (centre + ahead) - spread_north * rise
                flux = flux + weight_north * jnp.where(forth_north, rise_behind, rise_ahead)
                flux = flux - tilt_north * (slant + vertical[q, k, pl.ds(row + 1, 8)])
                flux = jnp.where(open_north, flux, 0.0)
                flux_north[q, pl.ds(row, 8)] = flux
                result = centre - flux + flux_north[q, pl.ds(row - 1, 8)]
                ahead = along_lanes(centre, -1)
                rise = jnp.where(lane == 127, 0.0, ahead - centre)
                flux = half_east * (centre + ahead) - spread_east * rise
                flux = flux + weight_east * jnp.where(forth_east, along_lanes(rise, 1), along_lanes(rise, -1))
                flux = flux - tilt_east * (slant + along_lanes(slant, -1))
                flux = jnp.where(open_east, flux, 0.0)
                interim = result - flux + along_lanes(flux, 1)
                values[q] = (interim + above * values[q]) * inverse
                sweep[q, k, here] = values[q]
            state[t] = (below, factor, *values)

    def one_level(k, state):
        state = list(state)
        main(k, state)
        return tuple(state)

    lax.fori_loop(0, levels, one_level, ((zero,) * 4,) * tiles)

    for t in range(tiles):
        here = pl.ds(8 * t, 8)
        depth = floor[here]
        values = [zero, zero]
        for k in reversed(range(levels)):
            factor, wet = upper[k, here], depth > k
            for q in range(2):
                values[q] = sweep[q, k, here] + factor * values[q]
                solved[q, k, here] = jnp.where(wet, values[q], 0.0)

    for t in range(tiles):
        here = pl.ds(8 * t, 8)
        inverse, below = zero, zero
        for k in range(levels):
            taken = lane_level == k
            inverse = jnp.where(taken, along_lanes(pivot[k, here], 4 * k + 2), inverse)
            below = jnp.where(taken, along_lanes(rate[k, here], 4 * k + 2), below)
        packed[5, here] = inverse
        packed[6, here] = below
    for t in range(tiles):
        here = pl.ds(8 * t, 8)
        inverse, below = packed[5, here], packed[6, here]
        factors = (jnp.where(lane_level == 0, 0.0, along_lanes(below, 4)) * inverse, below * inverse)
        for i, (factor, side) in enumerate(zip(factors, (1, -1))):
            for base in (1, 5):
                product = factor
                for j in range(1, 5):
                    scan[i, (4 if base == 5 else 0) + j - 1, here] = product
                    if j < 4 or base == 1:
                        product = factor * along_lanes(product, side * 4 * base)
                factor = product

    for k in range(levels):
        for i, ref in enumerate((pivot, rate, upper)):
            source = max(k - 1, 0) if i == 1 else k
            row_factors[i, k] = of_rows(*(row_of(ref, source, r) for r in (rows - 2, rows - 1, 0, 1)))

    @pl.when(at_south)
    def _():
        from_south[...] = jnp.zeros(from_south.shape, f32)

    @pl.when(jnp.logical_not(at_south))
    def _():
        to_north.wait_recv()

    @pl.when(jnp.logical_not(at_north))
    def _():
        to_south.wait_recv()

    @pl.when(at_north)
    def _():
        to_facing.wait_recv()

    @pl.when(jnp.logical_and(at_north, other))
    def _():
        to_beside.wait_recv()

    @pl.when(jnp.logical_and(at_north, jnp.logical_not(other)))
    def _():
        from_beside[...] = beside_message[...]

    @pl.when(at_north)
    def _():
        index = (row_of(partner, lon) - 128 * facing + 128 * lons) & (128 * lons - 1)
        inside = index < 128
        index = index & 127
        extra = from_beside[...]
        for m in range(last + 1):
            facing_rows = jnp.take_along_axis(from_north[m], index, axis=1, mode="promise_in_bounds")
            beside_rows = jnp.take_along_axis(extra, (index + 2 * m) & 127, axis=1, mode="promise_in_bounds")
            found = jnp.where(inside, facing_rows, beside_rows)
            from_north[m] = jnp.where(
                sub_place < 2,
                jnp.where(sub_place == 0, along_rows(found, -3), along_rows(found, -1)),
                jnp.where(sub_place == 2, along_rows(found, 1), along_rows(found, 3)),
            )

    own_floor = of_rows(*(row_of(floor, r) for r in (rows - 2, rows - 1, 0, 1))).astype(f32)
    far_floor = of_rows(
        row_of(from_north, last, 2), row_of(from_north, last, 3), row_of(from_south, last, 0), row_of(from_south, last, 1)
    )
    high = sub_place >= 2

    def own_rows(k):
        lo = jnp.where(sub < 2, cells[0, k, pl.ds(OFF + rows - 2, 8)], cells[0, k, pl.ds(OFF - 2, 8)])
        hi = jnp.where(sub < 6, cells[1, k, pl.ds(OFF + rows - 6, 8)], cells[1, k, pl.ds(OFF - 6, 8)])
        return jnp.where(sub < 4, lo, hi)

    def far_rows(k):
        south, north = from_south[k // 2], from_north[k // 2]
        if k % 2 == 1:
            south, north = along_rows(south, 2), along_rows(north, -2)
        return jnp.where(high, south, north)

    near_floor, beyond_floor = jnp.where(high, far_floor, own_floor), jnp.where(high, own_floor, far_floor)
    near, beyond = [], []

    def row_vertical(values, depth, k):
        above = values[max(k - 1, 0)]
        below = jnp.where(depth > k + 1.0, values[k + 1], values[k]) if k + 1 < levels else values[k]
        return above - below

    value = zero
    for k in range(levels):
        while len(near) < min(k + 2, levels):
            own, far = own_rows(len(near)), far_rows(len(near))
            near.append(jnp.where(high, far, own))
            beyond.append(jnp.where(high, own, far))
        speed = of_rows(
            row_of(raw, 4, k, rows - 2),
            row_of(raw, 4, k, rows - 1),
            row_of(raw, 4, k, 0),
            row_of(from_south, last + 1 + k // 4, 2 * (k % 4)),
        )
        slope = jnp.where(high, row_of(from_south, last + 1 + k // 4, 2 * (k % 4) + 1), row_of(raw, 5, k, rows - 1))
        terms = edge_terms(
            sub_place,
            along_rows,
            float(k),
            near[k],
            beyond[k],
            near_floor,
            beyond_floor,
            row_vertical(near, near_floor, k),
            row_vertical(beyond, beyond_floor, k),
            speed,
            slope,
        )
        value = (terms + row_factors[1, k] * value if k > 0 else terms) * row_factors[0, k]
        fix_rows[k] = value
    value = zero
    for k in reversed(range(levels)):
        value = fix_rows[k] + row_factors[2, k] * value
        fix_rows[k] = jnp.where(own_floor > k, value, 0.0)

    to_east.wait_recv()
    to_west.wait_recv()

    def lane_vertical(values, depth):
        above = jnp.where(lane_level == 0, values, along_lanes(values, 4))
        return above - jnp.where(level_f + 1.0 < depth, along_lanes(values, -4), values)

    high = lane_place >= 2
    for t in range(tiles):
        here = pl.ds(8 * t, 8)
        tracers_west, speeds_west, tracers_east = from_west[0, here], from_west[1, here], from_east[here]
        own_floor = packed[4, here]
        floor_beyond = jnp.where(lane_place == 0, column(tracers_east, 104), column(tracers_east, 105))
        far_floor = jnp.where(high, along_lanes(speeds_west, 2), floor_beyond)
        near_floor, beyond_floor = jnp.where(high, far_floor, own_floor), jnp.where(high, own_floor, far_floor)
        speed = jnp.where(lane_place == 3, speeds_west, packed[2, here])
        slope = jnp.where(lane_place == 3, along_lanes(speeds_west, 1), packed[3, here])
        far = (
            jnp.where(high, tracers_west, tracers_east),
            jnp.where(high, along_lanes(tracers_west, 2), along_lanes(tracers_east, -2)),
        )
        for q in range(2):
            own = packed[q, here]
            near, beyond = jnp.where(high, far[q], own), jnp.where(high, own, far[q])
            terms = edge_terms(
                lane_place,
                along_lanes,
                level_f,
                near,
                beyond,
                near_floor,
                beyond_floor,
                lane_vertical(near, near_floor),
                lane_vertical(beyond, beyond_floor),
                speed,
                slope,
            )
            value = terms * packed[5, here]
            for i, side in enumerate((1, -1)):
                for base in (1, 5):
                    terms = [
                        scan[i, (4 if base == 5 else 0) + j - 1, here] * along_lanes(value, side * 4 * base * j)
                        for j in range(1, 5)
                    ]
                    value = (value + terms[0]) + (terms[1] + (terms[2] + terms[3]))
            fix_columns[q, here] = jnp.where(level_f < own_floor, value, 0.0)

    to_east.wait_send()
    to_west.wait_send()

    @pl.when(jnp.logical_not(at_south))
    def _():
        to_south.wait_send()

    @pl.when(jnp.logical_not(at_north))
    def _():
        to_north.wait_send()

    @pl.when(at_north)
    def _():
        to_facing.wait_send()

    @pl.when(jnp.logical_and(at_north, other))
    def _():
        to_beside.wait_send()


def finish_kernel(solved, fix_columns, fix_rows, temp_out, salt_out, result, store_sem):
    levels, rows = solved.shape[1:3]
    tiles = rows // 8
    lane = lax.broadcasted_iota(jnp.int32, (8, 128), 1)
    sub = lax.broadcasted_iota(jnp.int32, (8, 128), 0)
    edge = ((lane + 2) & 127) < 4
    outputs = (temp_out, salt_out)

    def store(t, q):
        here = pl.ds(pl.multiple_of(8 * t, 8), 8)
        return pltpu.make_async_copy(result.at[q, :, here], outputs[q].at[:, here], store_sem.at[q, t])

    def columns(t):
        here = pl.ds(pl.multiple_of(8 * t, 8), 8)
        for q in range(2):
            terms = fix_columns[q, here]
            for k in range(levels):
                result[q, k, here] = solved[q, k, here] + jnp.where(edge, along_lanes(terms, 126 - 4 * k), 0.0)

    def corners(t, wanted):
        here = pl.ds(8 * t, 8)
        for q in range(2):
            for k in range(levels):
                terms = along_rows(fix_rows[k], 2 if q else -2)
                result[q, k, here] = result[q, k, here] + jnp.where(wanted, terms, 0.0)

    def whole(t):
        columns(t)
        for q in range(2):
            store(t, q).start()

    for t, wanted in ((0, sub < 2), (tiles - 1, sub >= 6)):
        columns(t)
        corners(t, wanted)
        for q in range(2):
            store(t, q).start()

    @pl.loop(1, tiles - 1)
    def _(t):
        whole(t)

    for t in range(tiles):
        for q in range(2):
            store(t, q).wait()


def local(axes, *arguments):
    levels, rows, columns = arguments[0].shape
    partner = arguments[8].reshape(-1, columns)
    shape = (levels, rows, columns)
    padded = (2, levels, rows + 2 * OFF, columns)
    pairs = levels // 2 + 1
    north_tiles = pairs + (levels + 3) // 4
    placed = pl.BlockSpec(memory_space=pltpu.VMEM)
    solved, fix_columns, fix_rows = pl.pallas_call(
        functools.partial(step_kernel, axes),
        out_shape=(
            jax.ShapeDtypeStruct((2, *shape), f32),
            jax.ShapeDtypeStruct((2, rows, columns), f32),
            jax.ShapeDtypeStruct((levels, 8, columns), f32),
        ),
        in_specs=[pl.BlockSpec(memory_space=pl.ANY)] * 9,
        out_specs=[placed] * 3,
        scratch_shapes=[
            pltpu.VMEM((6, *shape), f32),
            pltpu.VMEM((levels - 1, rows, columns), f32),
            pltpu.VMEM((rows + OFF, columns), jnp.int32),
            pltpu.VMEM(partner.shape, jnp.int32),
            pltpu.VMEM(padded, f32),
            pltpu.VMEM(padded, f32),
            pltpu.VMEM((2, rows + OFF, columns), f32),
            pltpu.VMEM((2, *shape), f32),
            pltpu.VMEM(shape, f32),
            pltpu.VMEM(shape, f32),
            pltpu.VMEM(shape, f32),
            pltpu.VMEM((rows, columns), jnp.int32),
            pltpu.VMEM((rows, columns), jnp.int32),
            pltpu.VMEM((7, rows, columns), f32),
            pltpu.VMEM((2, 8, rows, columns), f32),
            pltpu.VMEM((3, levels, 8, columns), f32),
            pltpu.VMEM((2, rows, columns), f32),
            pltpu.VMEM((rows, columns), f32),
            pltpu.VMEM((north_tiles, 8, columns), f32),
            pltpu.VMEM((pairs, 8, columns), f32),
            pltpu.VMEM((8, columns), f32),
            pltpu.VMEM((2, rows, columns), f32),
            pltpu.VMEM((rows, columns), f32),
            pltpu.VMEM((north_tiles, 8, columns), f32),
            pltpu.VMEM((pairs, 8, columns), f32),
            pltpu.VMEM((8, columns), f32),
            pltpu.SemaphoreType.DMA((24,)),
            pltpu.SemaphoreType.DMA((6,)),
            pltpu.SemaphoreType.DMA((5,)),
        ],
        compiler_params=pltpu.CompilerParams(
            collective_id=0, has_side_effects=True, vmem_limit_bytes=40 * 2**20
        ),
        name="tracer_step",
    )(*[pltpu.with_memory_space_constraint(a, pltpu.HBM) for a in (*arguments[:8], partner)])
    return pl.pallas_call(
        finish_kernel,
        out_shape=(jax.ShapeDtypeStruct(shape, f32),) * 2,
        in_specs=[placed] * 3,
        out_specs=[pl.BlockSpec(memory_space=pl.ANY)] * 2,
        scratch_shapes=[
            pltpu.VMEM((2, *shape), f32),
            pltpu.SemaphoreType.DMA((2, rows // 8)),
        ],
        compiler_params=pltpu.CompilerParams(vmem_limit_bytes=16 * 2**20),
        name="tracer_finish",
    )(solved, fix_columns, fix_rows)


def solution(mesh):
    axes = (mesh.shape["lat"], mesh.shape["lon"])
    block = P(None, "lat", "lon")
    return jax.shard_map(
        functools.partial(local, axes),
        mesh=mesh,
        in_specs=(block,) * 7 + (P("lat", "lon"), P()),
        out_specs=(block, block),
        check_vma=False,
    )
```

```python
import functools

import jax
import jax.numpy as jnp
from jax import lax
from jax.experimental import pallas as pl
from jax.experimental.pallas import tpu as pltpu
from jax.sharding import PartitionSpec as P

isopycnal_rate = 0.1
MESH = pl.DeviceIdType.MESH
f32 = jnp.float32
OFF = 8


def along_lanes(x, shift):
    return pltpu.roll(x, shift % 128, 1)


def along_rows(x, shift):
    return pltpu.roll(x, shift % 8, 0)


def row_of(ref, *index):
    *lead, row = index
    return jnp.broadcast_to(ref[(*lead, pl.ds(row, 1), slice(None))], (8, 128))


def edge_terms(place, turn, level, near, beyond, near_floor, beyond_floor, near_vertical, beyond_vertical, speed, slope):
    high = place >= 2
    own_floor = jnp.where(high, beyond_floor, near_floor)
    behind = turn(near, 1)
    ahead = turn(beyond, 1)
    weight = jnp.abs(speed) * (1.0 / 6.0)
    full = 0.5 * speed * (near + ahead) - (weight + isopycnal_rate) * (ahead - near)
    full = full + weight * jnp.where(speed > 0, near - behind, beyond - ahead)
    full = full - (0.25 * isopycnal_rate) * slope * (near_vertical + turn(beyond_vertical, 1))
    full = jnp.where(level < jnp.minimum(near_floor, turn(beyond_floor, 1)), full, 0.0)
    part = weight * (beyond - turn(near, -1))
    part = jnp.where(jnp.where(high, speed, -speed) > 0, part, 0.0)
    part = jnp.where(level < jnp.minimum(own_floor, turn(own_floor, -1)), part, 0.0)
    flux = jnp.where((place & 1) == 1, full, part)
    at_west = jnp.where(place == 2, turn(flux, -1), jnp.where(place == 0, 0.0, turn(flux, 1)))
    return at_west - jnp.where(place == 3, 0.0, flux)


def step_kernel(
    axes,
    temp_hbm,
    salt_hbm,
    east_hbm,
    north_hbm,
    tilt_east_hbm,
    tilt_north_hbm,
    mix_hbm,
    floor_hbm,
    partner_hbm,
    solved,
    fix_columns,
    fix_rows,
    raw,
    mix,
    floor,
    partner,
    cells,
    vertical,
    flux_north,
    sweep,
    pivot,
    rate,
    upper,
    floor_east,
    floor_north,
    packed,
    scan,
    row_factors,
    east_message,
    west_message,
    north_message,
    south_message,
    beside_message,
    from_west,
    from_east,
    from_south,
    from_north,
    from_beside,
    load_sem,
    send_sem,
    recv_sem,
):
    lats, lons = axes
    levels, rows = mix.shape[0] + 1, mix.shape[1]
    tiles = rows // 8
    lat, lon = lax.axis_index("lat"), lax.axis_index("lon")
    at_south, at_north = lat == 0, lat == lats - 1
    east, west = lax.rem(lon + 1, lons), lax.rem(lon + lons - 1, lons)
    facing, beside = lons - 1 - lon, lax.rem(lons - lon, lons)
    other = beside != lon
    parts = 4 if tiles % 4 == 0 else 1
    part_rows = rows // parts

    barrier = pltpu.get_barrier_semaphore()

    def greet(target_lat, target_lon):
        pl.semaphore_signal(barrier, inc=1, device_id={"lat": target_lat, "lon": target_lon}, device_id_type=MESH)

    greet(lat, east)
    greet(lat, west)

    @pl.when(jnp.logical_not(at_south))
    def _():
        greet(lat - 1, lon)

    @pl.when(jnp.logical_not(at_north))
    def _():
        greet(lat + 1, lon)

    @pl.when(at_north)
    def _():
        greet(lat, facing)

    @pl.when(jnp.logical_and(at_north, other))
    def _():
        greet(lat, beside)

    def load(source, target, index):
        copy = pltpu.make_async_copy(source, target, load_sem.at[index])
        copy.start()
        return copy

    first_loads = [load(floor_hbm, floor.at[pl.ds(0, rows)], 0)]
    part_loads = []
    for p in range(parts):
        chunk = pl.ds(p * part_rows, part_rows)
        part_loads.append(
            [
                load(ref.at[:, chunk], raw.at[i, :, chunk], 4 + 4 * p + i)
                for i, ref in enumerate((temp_hbm, salt_hbm, east_hbm, tilt_east_hbm))
            ]
        )

    def send(source, target, index, target_lat, target_lon, receive):
        return pltpu.make_async_remote_copy(
            src_ref=source,
            dst_ref=target,
            send_sem=send_sem.at[index],
            recv_sem=recv_sem.at[receive],
            device_id={"lat": target_lat, "lon": target_lon},
            device_id_type=MESH,
        )

    rows_only = north_message.at[pl.ds(0, south_message.shape[0])]
    to_east = send(east_message, from_west, 0, lat, east, 0)
    to_west = send(west_message, from_east, 1, lat, west, 1)
    to_north = send(north_message, from_south, 2, lat + 1, lon, 2)
    to_south = send(south_message, from_north, 3, lat - 1, lon, 3)
    to_facing = send(rows_only, from_north, 4, lat, facing, 3)
    to_beside = send(beside_message, from_beside, 5, lat, beside, 4)

    lane = lax.broadcasted_iota(jnp.int32, (8, 128), 1)
    sub = lax.broadcasted_iota(jnp.int32, (8, 128), 0)
    lane_place, lane_level = lane & 3, lane >> 2
    level_f = lane_level.astype(f32)
    sub_place = sub & 3
    floor_lanes = (lane >> 1) == 52
    zero = jnp.zeros((8, 128), f32)

    def column(values, index):
        return jnp.broadcast_to(values[:, index : index + 1], (8, 128))

    def of_four(a, b, c, d):
        return jnp.where(lane_place < 2, jnp.where(lane_place == 0, a, b), jnp.where(lane_place == 2, c, d))

    def of_rows(a, b, c, d):
        return jnp.where(sub_place < 2, jnp.where(sub_place == 0, a, b), jnp.where(sub_place == 2, c, d))

    def prepare(at):
        here, padded = pl.ds(at, 8), pl.ds(at + OFF, 8)
        depth = floor[here]
        packs = [zero, zero, zero, zero]
        before, now = [None, None], [None, None]
        for k in range(levels + 1):
            if k < levels:
                wet = depth > k
                taken = lane_level == k
                values = [jnp.where(wet, raw[q, k, here], 0.0) for q in range(2)]
                values += [raw[q, k, here] for q in (2, 3)]
                for q in range(4):
                    packs[q] = jnp.where(taken, along_lanes(values[q], 4 * k + 2), packs[q])
                for q in range(2):
                    cells[q, k, padded] = values[q]
            for q in range(2):
                if k > 0:
                    below = jnp.where(wet, values[q], now[q]) if k < levels else now[q]
                    vertical[q, k - 1, padded] = (before[q] if k > 1 else now[q]) - below
                before[q], now[q] = now[q], values[q]
        depth_f = depth.astype(f32)
        own_floor = of_four(column(depth_f, 126), column(depth_f, 127), column(depth_f, 0), column(depth_f, 1))
        for q in range(4):
            packed[q, here] = packs[q]
        packed[4, here] = own_floor
        high = lane_place >= 2
        east_message[0, here] = jnp.where(high, along_lanes(packs[0], 2), packs[1])
        speeds = jnp.where(lane_place == 3, along_lanes(packs[2], 2), along_lanes(packs[3], 1))
        east_message[1, here] = jnp.where(high, speeds, own_floor)
        tracers = jnp.where(high, packs[1], along_lanes(packs[0], -2))
        west_message[here] = jnp.where(floor_lanes, along_lanes(depth_f, 104), tracers)
        floor_east[here] = jnp.where(lane == 127, 0, jnp.minimum(depth, along_lanes(depth, -1)))

    for copy in first_loads:
        copy.wait()
    for p in range(parts):
        for copy in part_loads[p]:
            copy.wait()
        if p == max(parts - 2, 0):
            north_loads = [load(north_hbm, raw.at[4], 20), load(tilt_north_hbm, raw.at[5], 21)]
            last_loads = [load(mix_hbm, mix, 22), load(partner_hbm, partner, 23)]

        @pl.loop(0, part_rows // 8)
        def _(t, p=p):
            prepare(pl.multiple_of(p * part_rows + 8 * t, 8))

    place = lax.rem(lon, lons // 2)
    patient = jnp.logical_or(place == 0, jnp.logical_and(at_north, place < 4))
    prompt = jnp.logical_not(patient)

    def meet():
        pl.semaphore_wait(barrier, jnp.where(at_south, 3, jnp.where(jnp.logical_and(at_north, other), 5, 4)))
        to_east.start()
        to_west.start()

    def send_fold(when):
        @pl.when(jnp.logical_and(at_north, when))
        def _():
            to_facing.start()

        @pl.when(jnp.logical_and(jnp.logical_and(at_north, other), when))
        def _():
            to_beside.start()

    def send_rows(when):
        @pl.when(jnp.logical_and(jnp.logical_not(at_south), when))
        def _():
            to_south.start()

        @pl.when(jnp.logical_and(jnp.logical_not(at_north), when))
        def _():
            to_north.start()

    pl.when(prompt)(meet)

    for copy in north_loads:
        copy.wait()
    last = levels // 2
    north_message[last] = zero
    south_message[last] = zero
    north_message[north_message.shape[0] - 1] = zero
    top, bottom = pl.ds(rows - 2, 2), pl.ds(0, 2)
    for k in range(levels):
        m, odd = k // 2, k % 2
        for q in range(2):
            north_message[m, pl.ds(4 * q + 2 - 2 * odd, 2)] = cells[q, k, pl.ds(OFF + rows - 2, 2)]
            south_message[m, pl.ds(4 * q + 2 * odd, 2)] = cells[q, k, pl.ds(OFF, 2)]
            north_message[last + 1 + k // 4, pl.ds(2 * (k % 4) + q, 1)] = raw[4 + q, k, pl.ds(rows - 1, 1)]
    north_message[last, pl.ds(0, 2)] = floor[top].astype(f32)
    south_message[last, pl.ds(2, 2)] = floor[bottom].astype(f32)

    @pl.when(at_north)
    def _():
        pack = zero
        for m in range(last + 1):
            pack = jnp.where((lane >> 1) == m, along_lanes(north_message[m], 2 * m), pack)
        beside_message[...] = pack

    send_fold(prompt)

    for t in range(tiles):
        both = jnp.minimum(floor[pl.ds(8 * t, 8)], floor[pl.ds(8 * t + 1, 8)])
        floor_north[pl.ds(8 * t, 8)] = both if t < tiles - 1 else jnp.where(sub == 7, 0, both)

    for copy in last_loads:
        copy.wait()

    for q in range(2):
        flux_north[q, pl.ds(0, OFF)] = zero

    def main(k, state):
        for t in range(tiles):
            here = pl.ds(8 * t, 8)
            depth = floor[here]
            open_east, open_north = floor_east[here] > k, floor_north[here] > k
            speed_east, speed_north = raw[2, k, here], raw[4, k, here]
            weight_east, weight_north = jnp.abs(speed_east) * (1.0 / 6.0), jnp.abs(speed_north) * (1.0 / 6.0)
            spread_east, spread_north = weight_east + isopycnal_rate, weight_north + isopycnal_rate
            half_east, half_north = 0.5 * speed_east, 0.5 * speed_north
            forth_east, forth_north = speed_east > 0, speed_north > 0
            tilt_east, tilt_north = (0.25 * isopycnal_rate) * raw[3, k, here], (0.25 * isopycnal_rate) * raw[5, k, here]
            above, above_factor, *values = state[t]
            below = jnp.where(depth > k + 1, mix[jnp.minimum(k, levels - 2), here], 0.0)
            inverse = 1.0 / (1.0 + above + below - above * above_factor)
            factor = below * inverse
            pivot[k, here] = inverse
            rate[k, here] = below
            upper[k, here] = factor
            for q in range(2):
                row = OFF + 8 * t
                centre = cells[q, k, pl.ds(row, 8)]
                slant = vertical[q, k, pl.ds(row, 8)]
                ahead, beyond = cells[q, k, pl.ds(row + 1, 8)], cells[q, k, pl.ds(row + 2, 8)]
                rise, rise_behind, rise_ahead = ahead - centre, centre - cells[q, k, pl.ds(row - 1, 8)], beyond - ahead
                if t == 0:
                    rise_behind = jnp.where(sub == 0, 0.0, rise_behind)
                if t == tiles - 1:
                    rise_ahead = jnp.where(sub >= 6, 0.0, rise_ahead)
                flux = half_north * (centre + ahead) - spread_north * rise
                flux = flux + weight_north * jnp.where(forth_north, rise_behind, rise_ahead)
                flux = flux - tilt_north * (slant + vertical[q, k, pl.ds(row + 1, 8)])
                flux = jnp.where(open_north, flux, 0.0)
                flux_north[q, pl.ds(row, 8)] = flux
                result = centre - flux + flux_north[q, pl.ds(row - 1, 8)]
                ahead = along_lanes(centre, -1)
                rise = jnp.where(lane == 127, 0.0, ahead - centre)
                flux = half_east * (centre + ahead) - spread_east * rise
                flux = flux + weight_east * jnp.where(forth_east, along_lanes(rise, 1), along_lanes(rise, -1))
                flux = flux - tilt_east * (slant + along_lanes(slant, -1))
                flux = jnp.where(open_east, flux, 0.0)
                interim = result - flux + along_lanes(flux, 1)
                values[q] = (interim + above * values[q]) * inverse
                sweep[q, k, here] = values[q]
            state[t] = (below, factor, *values)

    def one_level(k, state):
        state = list(state)
        main(k, state)
        return tuple(state)

    early, late = 8, 10
    state = lax.fori_loop(0, early, one_level, ((zero,) * 4,) * tiles)
    send_rows(prompt)
    state = lax.fori_loop(early, late, one_level, state)
    pl.when(patient)(meet)
    send_rows(patient)
    send_fold(patient)
    lax.fori_loop(late, levels, one_level, state)

    for t in range(tiles):
        here = pl.ds(8 * t, 8)
        depth = floor[here]
        values = [zero, zero]
        for k in reversed(range(levels)):
            factor, wet = upper[k, here], depth > k
            for q in range(2):
                values[q] = sweep[q, k, here] + factor * values[q]
                solved[q, k, here] = jnp.where(wet, values[q], 0.0)

    for t in range(tiles):
        here = pl.ds(8 * t, 8)
        inverse, below = zero, zero
        for k in range(levels):
            taken = lane_level == k
            inverse = jnp.where(taken, along_lanes(pivot[k, here], 4 * k + 2), inverse)
            below = jnp.where(taken, along_lanes(rate[k, here], 4 * k + 2), below)
        packed[5, here] = inverse
        packed[6, here] = below
    for t in range(tiles):
        here = pl.ds(8 * t, 8)
        inverse, below = packed[5, here], packed[6, here]
        factors = (jnp.where(lane_level == 0, 0.0, along_lanes(below, 4)) * inverse, below * inverse)
        for i, (factor, side) in enumerate(zip(factors, (1, -1))):
            for base in (1, 5):
                product = factor
                for j in range(1, 5):
                    scan[i, (4 if base == 5 else 0) + j - 1, here] = product
                    if j < 4 or base == 1:
                        product = factor * along_lanes(product, side * 4 * base)
                factor = product

    for k in range(levels):
        for i, ref in enumerate((pivot, rate, upper)):
            source = max(k - 1, 0) if i == 1 else k
            row_factors[i, k] = of_rows(*(row_of(ref, source, r) for r in (rows - 2, rows - 1, 0, 1)))

    @pl.when(at_south)
    def _():
        from_south[...] = jnp.zeros(from_south.shape, f32)

    @pl.when(jnp.logical_not(at_south))
    def _():
        to_north.wait_recv()

    @pl.when(jnp.logical_not(at_north))
    def _():
        to_south.wait_recv()

    @pl.when(at_north)
    def _():
        to_facing.wait_recv()

    @pl.when(jnp.logical_and(at_north, other))
    def _():
        to_beside.wait_recv()

    @pl.when(jnp.logical_and(at_north, jnp.logical_not(other)))
    def _():
        from_beside[...] = beside_message[...]

    @pl.when(at_north)
    def _():
        index = (row_of(partner, lon) - 128 * facing + 128 * lons) & (128 * lons - 1)
        inside = index < 128
        index = index & 127
        extra = from_beside[...]
        for m in range(last + 1):
            facing_rows = jnp.take_along_axis(from_north[m], index, axis=1, mode="promise_in_bounds")
            beside_rows = jnp.take_along_axis(extra, (index + 2 * m) & 127, axis=1, mode="promise_in_bounds")
            found = jnp.where(inside, facing_rows, beside_rows)
            from_north[m] = jnp.where(
                sub_place < 2,
                jnp.where(sub_place == 0, along_rows(found, -3), along_rows(found, -1)),
                jnp.where(sub_place == 2, along_rows(found, 1), along_rows(found, 3)),
            )

    own_floor = of_rows(*(row_of(floor, r) for r in (rows - 2, rows - 1, 0, 1))).astype(f32)
    far_floor = of_rows(
        row_of(from_north, last, 2), row_of(from_north, last, 3), row_of(from_south, last, 0), row_of(from_south, last, 1)
    )
    high = sub_place >= 2

    def own_rows(k):
        lo = jnp.where(sub < 2, cells[0, k, pl.ds(OFF + rows - 2, 8)], cells[0, k, pl.ds(OFF - 2, 8)])
        hi = jnp.where(sub < 6, cells[1, k, pl.ds(OFF + rows - 6, 8)], cells[1, k, pl.ds(OFF - 6, 8)])
        return jnp.where(sub < 4, lo, hi)

    def far_rows(k):
        south, north = from_south[k // 2], from_north[k // 2]
        if k % 2 == 1:
            south, north = along_rows(south, 2), along_rows(north, -2)
        return jnp.where(high, south, north)

    near_floor, beyond_floor = jnp.where(high, far_floor, own_floor), jnp.where(high, own_floor, far_floor)
    near, beyond = [], []

    def row_vertical(values, depth, k):
        above = values[max(k - 1, 0)]
        below = jnp.where(depth > k + 1.0, values[k + 1], values[k]) if k + 1 < levels else values[k]
        return above - below

    value = zero
    for k in range(levels):
        while len(near) < min(k + 2, levels):
            own, far = own_rows(len(near)), far_rows(len(near))
            near.append(jnp.where(high, far, own))
            beyond.append(jnp.where(high, own, far))
        speed = of_rows(
            row_of(raw, 4, k, rows - 2),
            row_of(raw, 4, k, rows - 1),
            row_of(raw, 4, k, 0),
            row_of(from_south, last + 1 + k // 4, 2 * (k % 4)),
        )
        slope = jnp.where(high, row_of(from_south, last + 1 + k // 4, 2 * (k % 4) + 1), row_of(raw, 5, k, rows - 1))
        terms = edge_terms(
            sub_place,
            along_rows,
            float(k),
            near[k],
            beyond[k],
            near_floor,
            beyond_floor,
            row_vertical(near, near_floor, k),
            row_vertical(beyond, beyond_floor, k),
            speed,
            slope,
        )
        value = (terms + row_factors[1, k] * value if k > 0 else terms) * row_factors[0, k]
        fix_rows[k] = value
    value = zero
    for k in reversed(range(levels)):
        value = fix_rows[k] + row_factors[2, k] * value
        fix_rows[k] = jnp.where(own_floor > k, value, 0.0)

    to_east.wait_recv()
    to_west.wait_recv()

    def lane_vertical(values, depth):
        above = jnp.where(lane_level == 0, values, along_lanes(values, 4))
        return above - jnp.where(level_f + 1.0 < depth, along_lanes(values, -4), values)

    high = lane_place >= 2
    for t in range(tiles):
        here = pl.ds(8 * t, 8)
        tracers_west, speeds_west, tracers_east = from_west[0, here], from_west[1, here], from_east[here]
        own_floor = packed[4, here]
        floor_beyond = jnp.where(lane_place == 0, column(tracers_east, 104), column(tracers_east, 105))
        far_floor = jnp.where(high, along_lanes(speeds_west, 2), floor_beyond)
        near_floor, beyond_floor = jnp.where(high, far_floor, own_floor), jnp.where(high, own_floor, far_floor)
        speed = jnp.where(lane_place == 3, speeds_west, packed[2, here])
        slope = jnp.where(lane_place == 3, along_lanes(speeds_west, 1), packed[3, here])
        far = (
            jnp.where(high, tracers_west, tracers_east),
            jnp.where(high, along_lanes(tracers_west, 2), along_lanes(tracers_east, -2)),
        )
        for q in range(2):
            own = packed[q, here]
            near, beyond = jnp.where(high, far[q], own), jnp.where(high, own, far[q])
            terms = edge_terms(
                lane_place,
                along_lanes,
                level_f,
                near,
                beyond,
                near_floor,
                beyond_floor,
                lane_vertical(near, near_floor),
                lane_vertical(beyond, beyond_floor),
                speed,
                slope,
            )
            value = terms * packed[5, here]
            for i, side in enumerate((1, -1)):
                for base in (1, 5):
                    terms = [
                        scan[i, (4 if base == 5 else 0) + j - 1, here] * along_lanes(value, side * 4 * base * j)
                        for j in range(1, 5)
                    ]
                    value = (value + terms[0]) + (terms[1] + (terms[2] + terms[3]))
            fix_columns[q, here] = jnp.where(level_f < own_floor, value, 0.0)

    to_east.wait_send()
    to_west.wait_send()

    @pl.when(jnp.logical_not(at_south))
    def _():
        to_south.wait_send()

    @pl.when(jnp.logical_not(at_north))
    def _():
        to_north.wait_send()

    @pl.when(at_north)
    def _():
        to_facing.wait_send()

    @pl.when(jnp.logical_and(at_north, other))
    def _():
        to_beside.wait_send()


def finish_kernel(solved, fix_columns, fix_rows, temp_out, salt_out, result, store_sem):
    levels, rows = solved.shape[1:3]
    tiles = rows // 8
    lane = lax.broadcasted_iota(jnp.int32, (8, 128), 1)
    sub = lax.broadcasted_iota(jnp.int32, (8, 128), 0)
    edge = ((lane + 2) & 127) < 4
    outputs = (temp_out, salt_out)

    def store(t, q):
        here = pl.ds(pl.multiple_of(8 * t, 8), 8)
        return pltpu.make_async_copy(result.at[q, :, here], outputs[q].at[:, here], store_sem.at[q, t])

    def columns(t):
        here = pl.ds(pl.multiple_of(8 * t, 8), 8)
        for q in range(2):
            terms = fix_columns[q, here]
            for k in range(levels):
                result[q, k, here] = solved[q, k, here] + jnp.where(edge, along_lanes(terms, 126 - 4 * k), 0.0)

    def corners(t, wanted):
        here = pl.ds(8 * t, 8)
        for q in range(2):
            for k in range(levels):
                terms = along_rows(fix_rows[k], 2 if q else -2)
                result[q, k, here] = result[q, k, here] + jnp.where(wanted, terms, 0.0)

    def whole(t):
        columns(t)
        for q in range(2):
            store(t, q).start()

    for t, wanted in ((0, sub < 2), (tiles - 1, sub >= 6)):
        columns(t)
        corners(t, wanted)
        for q in range(2):
            store(t, q).start()

    @pl.loop(1, tiles - 1)
    def _(t):
        whole(t)

    for t in range(tiles):
        for q in range(2):
            store(t, q).wait()


def local(axes, *arguments):
    levels, rows, columns = arguments[0].shape
    partner = arguments[8].reshape(-1, columns)
    shape = (levels, rows, columns)
    padded = (2, levels, rows + 2 * OFF, columns)
    pairs = levels // 2 + 1
    north_tiles = pairs + (levels + 3) // 4
    placed = pl.BlockSpec(memory_space=pltpu.VMEM)
    solved, fix_columns, fix_rows = pl.pallas_call(
        functools.partial(step_kernel, axes),
        out_shape=(
            jax.ShapeDtypeStruct((2, *shape), f32),
            jax.ShapeDtypeStruct((2, rows, columns), f32),
            jax.ShapeDtypeStruct((levels, 8, columns), f32),
        ),
        in_specs=[pl.BlockSpec(memory_space=pl.ANY)] * 9,
        out_specs=[placed] * 3,
        scratch_shapes=[
            pltpu.VMEM((6, *shape), f32),
            pltpu.VMEM((levels - 1, rows, columns), f32),
            pltpu.VMEM((rows + OFF, columns), jnp.int32),
            pltpu.VMEM(partner.shape, jnp.int32),
            pltpu.VMEM(padded, f32),
            pltpu.VMEM(padded, f32),
            pltpu.VMEM((2, rows + OFF, columns), f32),
            pltpu.VMEM((2, *shape), f32),
            pltpu.VMEM(shape, f32),
            pltpu.VMEM(shape, f32),
            pltpu.VMEM(shape, f32),
            pltpu.VMEM((rows, columns), jnp.int32),
            pltpu.VMEM((rows, columns), jnp.int32),
            pltpu.VMEM((7, rows, columns), f32),
            pltpu.VMEM((2, 8, rows, columns), f32),
            pltpu.VMEM((3, levels, 8, columns), f32),
            pltpu.VMEM((2, rows, columns), f32),
            pltpu.VMEM((rows, columns), f32),
            pltpu.VMEM((north_tiles, 8, columns), f32),
            pltpu.VMEM((pairs, 8, columns), f32),
            pltpu.VMEM((8, columns), f32),
            pltpu.VMEM((2, rows, columns), f32),
            pltpu.VMEM((rows, columns), f32),
            pltpu.VMEM((north_tiles, 8, columns), f32),
            pltpu.VMEM((pairs, 8, columns), f32),
            pltpu.VMEM((8, columns), f32),
            pltpu.SemaphoreType.DMA((24,)),
            pltpu.SemaphoreType.DMA((6,)),
            pltpu.SemaphoreType.DMA((5,)),
        ],
        compiler_params=pltpu.CompilerParams(
            collective_id=0, has_side_effects=True, vmem_limit_bytes=40 * 2**20
        ),
        name="tracer_step",
    )(*[pltpu.with_memory_space_constraint(a, pltpu.HBM) for a in (*arguments[:8], partner)])
    return pl.pallas_call(
        finish_kernel,
        out_shape=(jax.ShapeDtypeStruct(shape, f32),) * 2,
        in_specs=[placed] * 3,
        out_specs=[pl.BlockSpec(memory_space=pl.ANY)] * 2,
        scratch_shapes=[
            pltpu.VMEM((2, *shape), f32),
            pltpu.SemaphoreType.DMA((2, rows // 8)),
        ],
        compiler_params=pltpu.CompilerParams(vmem_limit_bytes=16 * 2**20),
        name="tracer_finish",
    )(solved, fix_columns, fix_rows)


def solution(mesh):
    axes = (mesh.shape["lat"], mesh.shape["lon"])
    block = P(None, "lat", "lon")
    return jax.shard_map(
        functools.partial(local, axes),
        mesh=mesh,
        in_specs=(block,) * 7 + (P("lat", "lon"), P()),
        out_specs=(block, block),
        check_vma=False,
    )
```

```python
import functools

import jax
import jax.numpy as jnp
from jax import lax
from jax.experimental import pallas as pl
from jax.experimental.pallas import tpu as pltpu
from jax.sharding import PartitionSpec as P

isopycnal_rate = 0.1
MESH = pl.DeviceIdType.MESH
f32 = jnp.float32
OFF = 8


def along_lanes(x, shift):
    return pltpu.roll(x, shift % 128, 1)


def along_rows(x, shift):
    return pltpu.roll(x, shift % 8, 0)


def row_of(ref, *index):
    *lead, row = index
    return jnp.broadcast_to(ref[(*lead, pl.ds(row, 1), slice(None))], (8, 128))


def edge_terms(
    place, turn, level, near, beyond, ahead, near_floor, beyond_floor, ahead_floor, near_vertical, ahead_vertical, speed, slope
):
    high = place >= 2
    own_floor = jnp.where(high, beyond_floor, near_floor)
    weight = jnp.abs(speed) * (1.0 / 6.0)
    full = 0.5 * speed * (near + ahead) - (weight + isopycnal_rate) * (ahead - near)
    full = full + weight * jnp.where(speed > 0, near - turn(near, 1), beyond - ahead)
    full = full - (0.25 * isopycnal_rate) * slope * (near_vertical + ahead_vertical)
    full = jnp.where(level < jnp.minimum(near_floor, ahead_floor), full, 0.0)
    part = weight * (beyond - turn(near, -1))
    part = jnp.where(jnp.where(high, speed, -speed) > 0, part, 0.0)
    part = jnp.where(level < jnp.minimum(own_floor, turn(own_floor, -1)), part, 0.0)
    flux = jnp.where((place & 1) == 1, full, part)
    at_west = jnp.where(place == 2, turn(flux, -1), jnp.where(place == 0, 0.0, turn(flux, 1)))
    return at_west - jnp.where(place == 3, 0.0, flux)


def step_kernel(
    axes,
    temp_hbm,
    salt_hbm,
    east_hbm,
    north_hbm,
    tilt_east_hbm,
    tilt_north_hbm,
    mix_hbm,
    floor_hbm,
    partner_hbm,
    solved,
    fix_columns,
    fix_rows,
    raw,
    mix,
    floor,
    partner,
    cells,
    vertical,
    moved,
    slants,
    flux_east,
    flux_north,
    sweep,
    pivot,
    rate,
    upper,
    floor_east,
    floor_north,
    packed,
    scan,
    row_factors,
    east_message,
    west_message,
    north_message,
    south_message,
    beside_message,
    from_west,
    from_east,
    from_south,
    from_north,
    from_beside,
    load_sem,
    send_sem,
    recv_sem,
):
    lats, lons = axes
    levels, rows = mix.shape[0] + 1, mix.shape[1]
    tiles = rows // 8
    lat, lon = lax.axis_index("lat"), lax.axis_index("lon")
    at_south, at_north = lat == 0, lat == lats - 1
    east, west = lax.rem(lon + 1, lons), lax.rem(lon + lons - 1, lons)
    facing, beside = lons - 1 - lon, lax.rem(lons - lon, lons)
    other = beside != lon
    parts = 4 if tiles % 4 == 0 else 1
    part_rows = rows // parts

    barrier = pltpu.get_barrier_semaphore()

    def greet(target_lat, target_lon):
        pl.semaphore_signal(barrier, inc=1, device_id={"lat": target_lat, "lon": target_lon}, device_id_type=MESH)

    greet(lat, east)
    greet(lat, west)

    @pl.when(jnp.logical_not(at_south))
    def _():
        greet(lat - 1, lon)

    @pl.when(jnp.logical_not(at_north))
    def _():
        greet(lat + 1, lon)

    @pl.when(at_north)
    def _():
        greet(lat, facing)

    @pl.when(jnp.logical_and(at_north, other))
    def _():
        greet(lat, beside)

    def load(source, target, index):
        copy = pltpu.make_async_copy(source, target, load_sem.at[index])
        copy.start()
        return copy

    first_loads = [load(floor_hbm, floor.at[pl.ds(0, rows)], 0)]
    part_loads = []
    for p in range(parts):
        chunk = pl.ds(p * part_rows, part_rows)
        part_loads.append(
            [
                load(ref.at[:, chunk], raw.at[i, :, chunk], 4 + 4 * p + i)
                for i, ref in enumerate((temp_hbm, salt_hbm, east_hbm, tilt_east_hbm))
            ]
        )

    def send(source, target, index, target_lat, target_lon, receive):
        return pltpu.make_async_remote_copy(
            src_ref=source,
            dst_ref=target,
            send_sem=send_sem.at[index],
            recv_sem=recv_sem.at[receive],
            device_id={"lat": target_lat, "lon": target_lon},
            device_id_type=MESH,
        )

    rows_only = north_message.at[pl.ds(0, south_message.shape[0])]
    to_east = send(east_message, from_west, 0, lat, east, 0)
    to_west = send(west_message, from_east, 1, lat, west, 1)
    to_north = send(north_message, from_south, 2, lat + 1, lon, 2)
    to_south = send(south_message, from_north, 3, lat - 1, lon, 3)
    to_facing = send(rows_only, from_north, 4, lat, facing, 3)
    to_beside = send(beside_message, from_beside, 5, lat, beside, 4)

    lane = lax.broadcasted_iota(jnp.int32, (8, 128), 1)
    sub = lax.broadcasted_iota(jnp.int32, (8, 128), 0)
    lane_place, lane_level = lane & 3, lane >> 2
    level_f = lane_level.astype(f32)
    sub_place = sub & 3
    floor_lanes = (lane >> 1) == 52
    zero = jnp.zeros((8, 128), f32)

    def column(values, index):
        return jnp.broadcast_to(values[:, index : index + 1], (8, 128))

    def of_four(a, b, c, d):
        return jnp.where(lane_place < 2, jnp.where(lane_place == 0, a, b), jnp.where(lane_place == 2, c, d))

    def of_rows(a, b, c, d):
        return jnp.where(sub_place < 2, jnp.where(sub_place == 0, a, b), jnp.where(sub_place == 2, c, d))

    def prepare(at):
        here, padded = pl.ds(at, 8), pl.ds(at + OFF, 8)
        depth = floor[here]
        packs = [zero, zero, zero, zero]
        before, now = [None, None], [None, None]
        for k in range(levels + 1):
            if k < levels:
                wet = depth > k
                taken = lane_level == k
                values = [jnp.where(wet, raw[q, k, here], 0.0) for q in range(2)]
                values += [raw[q, k, here] for q in (2, 3)]
                for q in range(4):
                    packs[q] = jnp.where(taken, along_lanes(values[q], 4 * k + 2), packs[q])
                for q in range(2):
                    cells[q, k, padded] = values[q]
            for q in range(2):
                if k > 0:
                    below = jnp.where(wet, values[q], now[q]) if k < levels else now[q]
                    vertical[q, k - 1, padded] = (before[q] if k > 1 else now[q]) - below
                before[q], now[q] = now[q], values[q]
        depth_f = depth.astype(f32)
        own_floor = of_four(column(depth_f, 126), column(depth_f, 127), column(depth_f, 0), column(depth_f, 1))
        for q in range(4):
            packed[q, here] = packs[q]
        packed[4, here] = own_floor
        high = lane_place >= 2
        east_message[0, here] = jnp.where(high, along_lanes(packs[0], 2), packs[1])
        speeds = jnp.where(lane_place == 3, along_lanes(packs[2], 2), along_lanes(packs[3], 1))
        east_message[1, here] = jnp.where(high, speeds, own_floor)
        tracers = jnp.where(high, packs[1], along_lanes(packs[0], -2))
        west_message[here] = jnp.where(floor_lanes, along_lanes(depth_f, 104), tracers)
        floor_east[here] = jnp.where(lane == 127, 0, jnp.minimum(depth, along_lanes(depth, -1)))

    for copy in first_loads:
        copy.wait()
    for p in range(parts):
        for copy in part_loads[p]:
            copy.wait()
        if p == max(parts - 2, 0):
            north_loads = [load(north_hbm, raw.at[4], 20), load(tilt_north_hbm, raw.at[5], 21)]
            last_loads = [load(mix_hbm, mix, 22), load(partner_hbm, partner, 23)]

        for t in range(part_rows // 8):
            prepare(p * part_rows + 8 * t)

    place = lax.rem(lon, lons // 2)
    patient = jnp.logical_or(place == 0, jnp.logical_and(at_north, place == 1))
    between = jnp.logical_and(at_north, jnp.logical_or(place == 2, place == 3))
    prompt = jnp.logical_not(jnp.logical_or(patient, between))

    def meet():
        pl.semaphore_wait(barrier, jnp.where(at_south, 3, jnp.where(jnp.logical_and(at_north, other), 5, 4)))
        to_east.start()
        to_west.start()

    def send_fold(when):
        @pl.when(jnp.logical_and(at_north, when))
        def _():
            to_facing.start()

        @pl.when(jnp.logical_and(jnp.logical_and(at_north, other), when))
        def _():
            to_beside.start()

    def send_rows(when):
        @pl.when(jnp.logical_and(jnp.logical_not(at_south), when))
        def _():
            to_south.start()

        @pl.when(jnp.logical_and(jnp.logical_not(at_north), when))
        def _():
            to_north.start()

    pl.when(prompt)(meet)

    for copy in north_loads:
        copy.wait()
    last = levels // 2
    north_message[last] = zero
    south_message[last] = zero
    north_message[north_message.shape[0] - 1] = zero
    top, bottom = pl.ds(rows - 2, 2), pl.ds(0, 2)
    for k in range(levels):
        m, odd = k // 2, k % 2
        for q in range(2):
            north_message[m, pl.ds(4 * q + 2 - 2 * odd, 2)] = cells[q, k, pl.ds(OFF + rows - 2, 2)]
            south_message[m, pl.ds(4 * q + 2 * odd, 2)] = cells[q, k, pl.ds(OFF, 2)]
            north_message[last + 1 + k // 4, pl.ds(2 * (k % 4) + q, 1)] = raw[4 + q, k, pl.ds(rows - 1, 1)]
    north_message[last, pl.ds(0, 2)] = floor[top].astype(f32)
    south_message[last, pl.ds(2, 2)] = floor[bottom].astype(f32)

    @pl.when(at_north)
    def _():
        pack = zero
        for m in range(last + 1):
            pack = jnp.where((lane >> 1) == m, along_lanes(north_message[m], 2 * m), pack)
        beside_message[...] = pack

    send_fold(prompt)

    for t in range(tiles):
        both = jnp.minimum(floor[pl.ds(8 * t, 8)], floor[pl.ds(8 * t + 1, 8)])
        floor_north[pl.ds(8 * t, 8)] = both if t < tiles - 1 else jnp.where(sub == 7, 0, both)

    for copy in last_loads:
        copy.wait()

    for q in range(2):
        flux_north[q, pl.ds(0, OFF)] = zero

    def shift(k):
        for t in range(tiles):
            here, padded = pl.ds(8 * t, 8), pl.ds(OFF + 8 * t, 8)
            for q in range(2):
                slant = vertical[q, k, padded]
                moved[q, k, here] = along_lanes(cells[q, k, padded], -1)
                slants[q, k, here] = slant + along_lanes(slant, -1)

    def east_faces(k):
        for t in range(tiles):
            here, padded = pl.ds(8 * t, 8), pl.ds(OFF + 8 * t, 8)
            opened, speed = floor_east[here] > k, raw[2, k, here]
            weight, half, forth = jnp.abs(speed) * (1.0 / 6.0), 0.5 * speed, speed > 0
            spread, tilt = weight + isopycnal_rate, (0.25 * isopycnal_rate) * raw[3, k, here]
            for q in range(2):
                centre, ahead = cells[q, k, padded], moved[q, k, here]
                rise = jnp.where(lane == 127, 0.0, ahead - centre)
                flux = half * (centre + ahead) - spread * rise
                flux = flux + weight * jnp.where(forth, along_lanes(rise, 1), along_lanes(rise, -1))
                flux = flux - tilt * slants[q, k, here]
                flux_east[q, k, here] = jnp.where(opened, flux, 0.0)

    def eliminate(k, state):
        for t in range(tiles):
            here = pl.ds(8 * t, 8)
            depth = floor[here]
            opened, speed = floor_north[here] > k, raw[4, k, here]
            weight, half, forth = jnp.abs(speed) * (1.0 / 6.0), 0.5 * speed, speed > 0
            spread, tilt = weight + isopycnal_rate, (0.25 * isopycnal_rate) * raw[5, k, here]
            above, above_factor, *values = state[t]
            below = jnp.where(depth > k + 1, mix[jnp.minimum(k, levels - 2), here], 0.0)
            inverse = 1.0 / (1.0 + above + below - above * above_factor)
            factor = below * inverse
            pivot[k, here] = inverse
            rate[k, here] = below
            upper[k, here] = factor
            for q in range(2):
                row = OFF + 8 * t
                centre = cells[q, k, pl.ds(row, 8)]
                ahead, beyond = cells[q, k, pl.ds(row + 1, 8)], cells[q, k, pl.ds(row + 2, 8)]
                rise, rise_behind, rise_ahead = ahead - centre, centre - cells[q, k, pl.ds(row - 1, 8)], beyond - ahead
                if t == 0:
                    rise_behind = jnp.where(sub == 0, 0.0, rise_behind)
                if t == tiles - 1:
                    rise_ahead = jnp.where(sub >= 6, 0.0, rise_ahead)
                flux = half * (centre + ahead) - spread * rise
                flux = flux + weight * jnp.where(forth, rise_behind, rise_ahead)
                flux = flux - tilt * (vertical[q, k, pl.ds(row, 8)] + vertical[q, k, pl.ds(row + 1, 8)])
                flux = jnp.where(opened, flux, 0.0)
                flux_north[q, pl.ds(row, 8)] = flux
                interim = centre - flux + flux_north[q, pl.ds(row - 1, 8)]
                flux = flux_east[q, k, here]
                interim = interim - flux + along_lanes(flux, 1)
                values[q] = (interim + above * values[q]) * inverse
                sweep[q, k, here] = values[q]
            state[t] = (below, factor, *values)

    shift(0)
    shift(min(1, levels - 1))
    east_faces(0)

    def one_level(k, state):
        state = list(state)
        eliminate(k, state)
        east_faces(jnp.minimum(k + 1, levels - 1))
        shift(jnp.minimum(k + 2, levels - 1))
        return tuple(state)

    early, late = 6, 10
    state = lax.fori_loop(0, early, one_level, ((zero,) * 4,) * tiles)
    pl.when(between)(meet)
    send_fold(between)
    send_rows(jnp.logical_not(patient))
    state = lax.fori_loop(early, late, one_level, state)
    pl.when(patient)(meet)
    send_fold(patient)
    send_rows(patient)
    lax.fori_loop(late, levels, one_level, state)

    for t in range(tiles):
        here = pl.ds(8 * t, 8)
        depth = floor[here]
        values = [zero, zero]
        for k in reversed(range(levels)):
            factor, wet = upper[k, here], depth > k
            for q in range(2):
                values[q] = sweep[q, k, here] + factor * values[q]
                solved[q, k, here] = jnp.where(wet, values[q], 0.0)

    for t in range(tiles):
        here = pl.ds(8 * t, 8)
        inverse, below = zero, zero
        for k in range(levels):
            taken = lane_level == k
            inverse = jnp.where(taken, along_lanes(pivot[k, here], 4 * k + 2), inverse)
            below = jnp.where(taken, along_lanes(rate[k, here], 4 * k + 2), below)
        packed[5, here] = inverse
        packed[6, here] = below
    for t in range(tiles):
        here = pl.ds(8 * t, 8)
        inverse, below = packed[5, here], packed[6, here]
        factors = (jnp.where(lane_level == 0, 0.0, along_lanes(below, 4)) * inverse, below * inverse)
        for i, (one, side) in enumerate(zip(factors, (4, -4))):
            two = one * along_lanes(one, side)
            four = two * along_lanes(two, 2 * side)
            five = one * along_lanes(four, side)
            ten = five * along_lanes(five, 5 * side)
            products = (one, two, one * along_lanes(two, side), four)
            products += (five, ten, five * along_lanes(ten, 5 * side), ten * along_lanes(ten, 10 * side))
            for j, product in enumerate(products):
                scan[i, j, here] = product

    for k in range(levels):
        for i, ref in enumerate((pivot, rate, upper)):
            source = max(k - 1, 0) if i == 1 else k
            row_factors[i, k] = of_rows(*(row_of(ref, source, r) for r in (rows - 2, rows - 1, 0, 1)))

    @pl.when(at_south)
    def _():
        from_south[...] = jnp.zeros(from_south.shape, f32)

    @pl.when(jnp.logical_not(at_south))
    def _():
        to_north.wait_recv()

    @pl.when(jnp.logical_not(at_north))
    def _():
        to_south.wait_recv()

    @pl.when(at_north)
    def _():
        to_facing.wait_recv()

    @pl.when(jnp.logical_and(at_north, other))
    def _():
        to_beside.wait_recv()

    @pl.when(jnp.logical_and(at_north, jnp.logical_not(other)))
    def _():
        from_beside[...] = beside_message[...]

    @pl.when(at_north)
    def _():
        index = (row_of(partner, lon) - 128 * facing + 128 * lons) & (128 * lons - 1)
        inside = index < 128
        index = index & 127
        extra = from_beside[...]
        for m in range(last + 1):
            facing_rows = jnp.take_along_axis(from_north[m], index, axis=1, mode="promise_in_bounds")
            beside_rows = jnp.take_along_axis(extra, (index + 2 * m) & 127, axis=1, mode="promise_in_bounds")
            found = jnp.where(inside, facing_rows, beside_rows)
            from_north[m] = jnp.where(
                sub_place < 2,
                jnp.where(sub_place == 0, along_rows(found, -3), along_rows(found, -1)),
                jnp.where(sub_place == 2, along_rows(found, 1), along_rows(found, 3)),
            )

    own_floor = of_rows(*(row_of(floor, r) for r in (rows - 2, rows - 1, 0, 1))).astype(f32)
    far_floor = of_rows(
        row_of(from_north, last, 2), row_of(from_north, last, 3), row_of(from_south, last, 0), row_of(from_south, last, 1)
    )
    high = sub_place >= 2

    def own_rows(k):
        lo = jnp.where(sub < 2, cells[0, k, pl.ds(OFF + rows - 2, 8)], cells[0, k, pl.ds(OFF - 2, 8)])
        hi = jnp.where(sub < 6, cells[1, k, pl.ds(OFF + rows - 6, 8)], cells[1, k, pl.ds(OFF - 6, 8)])
        return jnp.where(sub < 4, lo, hi)

    def far_rows(k):
        south, north = from_south[k // 2], from_north[k // 2]
        if k % 2 == 1:
            south, north = along_rows(south, 2), along_rows(north, -2)
        return jnp.where(high, south, north)

    near_floor, beyond_floor = jnp.where(high, far_floor, own_floor), jnp.where(high, own_floor, far_floor)
    ahead_floor = along_rows(beyond_floor, 1)
    near, beyond, ahead = [], [], []

    def row_vertical(values, depth, k):
        above = values[max(k - 1, 0)]
        below = jnp.where(depth > k + 1.0, values[k + 1], values[k]) if k + 1 < levels else values[k]
        return above - below

    value = zero
    for k in range(levels):
        while len(near) < min(k + 2, levels):
            own, far = own_rows(len(near)), far_rows(len(near))
            near.append(jnp.where(high, far, own))
            beyond.append(jnp.where(high, own, far))
            ahead.append(along_rows(beyond[-1], 1))
        speed = of_rows(
            row_of(raw, 4, k, rows - 2),
            row_of(raw, 4, k, rows - 1),
            row_of(raw, 4, k, 0),
            row_of(from_south, last + 1 + k // 4, 2 * (k % 4)),
        )
        slope = jnp.where(high, row_of(from_south, last + 1 + k // 4, 2 * (k % 4) + 1), row_of(raw, 5, k, rows - 1))
        terms = edge_terms(
            sub_place,
            along_rows,
            float(k),
            near[k],
            beyond[k],
            ahead[k],
            near_floor,
            beyond_floor,
            ahead_floor,
            row_vertical(near, near_floor, k),
            row_vertical(ahead, ahead_floor, k),
            speed,
            slope,
        )
        value = (terms + row_factors[1, k] * value if k > 0 else terms) * row_factors[0, k]
        fix_rows[k] = value
    value = zero
    for k in reversed(range(levels)):
        value = fix_rows[k] + row_factors[2, k] * value
        fix_rows[k] = jnp.where(own_floor > k, value, 0.0)

    to_east.wait_recv()
    to_west.wait_recv()

    def lane_vertical(values, here, depth, shift):
        above = jnp.where(lane_level == 0, here, along_lanes(values, shift + 4))
        return above - jnp.where(level_f + 1.0 < depth, along_lanes(values, shift - 4), here)

    high = lane_place >= 2
    for t in range(tiles):
        here = pl.ds(8 * t, 8)
        tracers_west, speeds_west, tracers_east = from_west[0, here], from_west[1, here], from_east[here]
        own_floor = packed[4, here]
        floor_beyond = jnp.where(lane_place == 0, column(tracers_east, 104), column(tracers_east, 105))
        far_floor = jnp.where(high, along_lanes(speeds_west, 2), floor_beyond)
        near_floor, beyond_floor = jnp.where(high, far_floor, own_floor), jnp.where(high, own_floor, far_floor)
        ahead_floor = along_lanes(beyond_floor, 1)
        speed = jnp.where(lane_place == 3, speeds_west, packed[2, here])
        slope = jnp.where(lane_place == 3, along_lanes(speeds_west, 1), packed[3, here])
        far = (
            jnp.where(high, tracers_west, tracers_east),
            jnp.where(high, along_lanes(tracers_west, 2), along_lanes(tracers_east, -2)),
        )
        for q in range(2):
            own = packed[q, here]
            near, beyond = jnp.where(high, far[q], own), jnp.where(high, own, far[q])
            ahead = along_lanes(beyond, 1)
            terms = edge_terms(
                lane_place,
                along_lanes,
                level_f,
                near,
                beyond,
                ahead,
                near_floor,
                beyond_floor,
                ahead_floor,
                lane_vertical(near, near, near_floor, 0),
                lane_vertical(beyond, ahead, ahead_floor, 1),
                speed,
                slope,
            )
            value = terms * packed[5, here]
            for i, side in enumerate((1, -1)):
                for base in (1, 5):
                    terms = [
                        scan[i, (4 if base == 5 else 0) + j - 1, here] * along_lanes(value, side * 4 * base * j)
                        for j in range(1, 5)
                    ]
                    value = (value + terms[0]) + (terms[1] + (terms[2] + terms[3]))
            fix_columns[q, here] = jnp.where(level_f < own_floor, value, 0.0)

    to_east.wait_send()
    to_west.wait_send()

    @pl.when(jnp.logical_not(at_south))
    def _():
        to_south.wait_send()

    @pl.when(jnp.logical_not(at_north))
    def _():
        to_north.wait_send()

    @pl.when(at_north)
    def _():
        to_facing.wait_send()

    @pl.when(jnp.logical_and(at_north, other))
    def _():
        to_beside.wait_send()


def finish_kernel(solved, fix_columns, fix_rows, temp_out, salt_out, result, store_sem):
    levels, rows = solved.shape[1:3]
    tiles = rows // 8
    lane = lax.broadcasted_iota(jnp.int32, (8, 128), 1)
    sub = lax.broadcasted_iota(jnp.int32, (8, 128), 0)
    edge = ((lane + 2) & 127) < 4
    outputs = (temp_out, salt_out)

    def store(t, q):
        here = pl.ds(8 * t, 8)
        return pltpu.make_async_copy(result.at[q, :, here], outputs[q].at[:, here], store_sem.at[q, t])

    def columns(t):
        here = pl.ds(8 * t, 8)
        for q in range(2):
            terms = fix_columns[q, here]
            for k in range(levels):
                result[q, k, here] = solved[q, k, here] + jnp.where(edge, along_lanes(terms, 126 - 4 * k), 0.0)

    def corners(t, wanted):
        here = pl.ds(8 * t, 8)
        for q in range(2):
            for k in range(levels):
                terms = along_rows(fix_rows[k], 2 if q else -2)
                result[q, k, here] = result[q, k, here] + jnp.where(wanted, terms, 0.0)

    for t in range(tiles):
        columns(t)
        if t == 0 or t == tiles - 1:
            corners(t, sub < 2 if t == 0 else sub >= 6)
        for q in range(2):
            store(t, q).start()

    for t in range(tiles):
        for q in range(2):
            store(t, q).wait()


def local(axes, *arguments):
    levels, rows, columns = arguments[0].shape
    partner = arguments[8].reshape(-1, columns)
    shape = (levels, rows, columns)
    padded = (2, levels, rows + 2 * OFF, columns)
    pairs = levels // 2 + 1
    north_tiles = pairs + (levels + 3) // 4
    placed = pl.BlockSpec(memory_space=pltpu.VMEM)
    solved, fix_columns, fix_rows = pl.pallas_call(
        functools.partial(step_kernel, axes),
        out_shape=(
            jax.ShapeDtypeStruct((2, *shape), f32),
            jax.ShapeDtypeStruct((2, rows, columns), f32),
            jax.ShapeDtypeStruct((levels, 8, columns), f32),
        ),
        in_specs=[pl.BlockSpec(memory_space=pl.ANY)] * 9,
        out_specs=[placed] * 3,
        scratch_shapes=[
            pltpu.VMEM((6, *shape), f32),
            pltpu.VMEM((levels - 1, rows, columns), f32),
            pltpu.VMEM((rows + OFF, columns), jnp.int32),
            pltpu.VMEM(partner.shape, jnp.int32),
            pltpu.VMEM(padded, f32),
            pltpu.VMEM(padded, f32),
            pltpu.VMEM((2, *shape), f32),
            pltpu.VMEM((2, *shape), f32),
            pltpu.VMEM((2, *shape), f32),
            pltpu.VMEM((2, rows + OFF, columns), f32),
            pltpu.VMEM((2, *shape), f32),
            pltpu.VMEM(shape, f32),
            pltpu.VMEM(shape, f32),
            pltpu.VMEM(shape, f32),
            pltpu.VMEM((rows, columns), jnp.int32),
            pltpu.VMEM((rows, columns), jnp.int32),
            pltpu.VMEM((7, rows, columns), f32),
            pltpu.VMEM((2, 8, rows, columns), f32),
            pltpu.VMEM((3, levels, 8, columns), f32),
            pltpu.VMEM((2, rows, columns), f32),
            pltpu.VMEM((rows, columns), f32),
            pltpu.VMEM((north_tiles, 8, columns), f32),
            pltpu.VMEM((pairs, 8, columns), f32),
            pltpu.VMEM((8, columns), f32),
            pltpu.VMEM((2, rows, columns), f32),
            pltpu.VMEM((rows, columns), f32),
            pltpu.VMEM((north_tiles, 8, columns), f32),
            pltpu.VMEM((pairs, 8, columns), f32),
            pltpu.VMEM((8, columns), f32),
            pltpu.SemaphoreType.DMA((24,)),
            pltpu.SemaphoreType.DMA((6,)),
            pltpu.SemaphoreType.DMA((5,)),
        ],
        compiler_params=pltpu.CompilerParams(
            collective_id=0, has_side_effects=True, vmem_limit_bytes=40 * 2**20
        ),
        name="tracer_step",
    )(*[pltpu.with_memory_space_constraint(a, pltpu.HBM) for a in (*arguments[:8], partner)])
    return pl.pallas_call(
        finish_kernel,
        out_shape=(jax.ShapeDtypeStruct(shape, f32),) * 2,
        in_specs=[placed] * 3,
        out_specs=[pl.BlockSpec(memory_space=pl.ANY)] * 2,
        scratch_shapes=[
            pltpu.VMEM((2, *shape), f32),
            pltpu.SemaphoreType.DMA((2, rows // 8)),
        ],
        compiler_params=pltpu.CompilerParams(vmem_limit_bytes=16 * 2**20),
        name="tracer_finish",
    )(solved, fix_columns, fix_rows)


def solution(mesh):
    axes = (mesh.shape["lat"], mesh.shape["lon"])
    block = P(None, "lat", "lon")
    return jax.shard_map(
        functools.partial(local, axes),
        mesh=mesh,
        in_specs=(block,) * 7 + (P("lat", "lon"), P()),
        out_specs=(block, block),
        check_vma=False,
    )
```

```python
import functools

import jax
import jax.numpy as jnp
from jax import lax
from jax.experimental import pallas as pl
from jax.experimental.pallas import tpu as pltpu
from jax.sharding import PartitionSpec as P

isopycnal_rate = 0.1
MESH = pl.DeviceIdType.MESH
f32 = jnp.float32
OFF = 8


def along_lanes(x, shift):
    return pltpu.roll(x, shift % 128, 1)


def along_rows(x, shift):
    return pltpu.roll(x, shift % 8, 0)


def row_of(ref, *index):
    *lead, row = index
    return jnp.broadcast_to(ref[(*lead, pl.ds(row, 1), slice(None))], (8, 128))


def edge_terms(
    place, turn, level, near, beyond, ahead, near_floor, beyond_floor, ahead_floor, near_vertical, ahead_vertical, speed, slope
):
    high = place >= 2
    own_floor = jnp.where(high, beyond_floor, near_floor)
    weight = jnp.abs(speed) * (1.0 / 6.0)
    full = 0.5 * speed * (near + ahead) - (weight + isopycnal_rate) * (ahead - near)
    full = full + weight * jnp.where(speed > 0, near - turn(near, 1), beyond - ahead)
    full = full - (0.25 * isopycnal_rate) * slope * (near_vertical + ahead_vertical)
    full = jnp.where(level < jnp.minimum(near_floor, ahead_floor), full, 0.0)
    part = weight * (beyond - turn(near, -1))
    part = jnp.where(jnp.where(high, speed, -speed) > 0, part, 0.0)
    part = jnp.where(level < jnp.minimum(own_floor, turn(own_floor, -1)), part, 0.0)
    flux = jnp.where((place & 1) == 1, full, part)
    at_west = jnp.where(place == 2, turn(flux, -1), jnp.where(place == 0, 0.0, turn(flux, 1)))
    return at_west - jnp.where(place == 3, 0.0, flux)


def step_kernel(
    axes,
    temp_hbm,
    salt_hbm,
    east_hbm,
    north_hbm,
    tilt_east_hbm,
    tilt_north_hbm,
    mix_hbm,
    floor_hbm,
    partner_hbm,
    solved,
    fix_columns,
    fix_rows,
    raw,
    mix,
    floor,
    partner,
    cells,
    vertical,
    moved,
    slants,
    flux_east,
    flux_north,
    sweep,
    pivot,
    rate,
    upper,
    floor_east,
    floor_north,
    packed,
    scan,
    row_factors,
    east_message,
    west_message,
    north_message,
    south_message,
    beside_message,
    from_west,
    from_east,
    from_south,
    from_north,
    from_beside,
    load_sem,
    send_sem,
    recv_sem,
):
    lats, lons = axes
    levels, rows = mix.shape[0] + 1, mix.shape[1]
    tiles = rows // 8
    lat, lon = lax.axis_index("lat"), lax.axis_index("lon")
    at_south, at_north = lat == 0, lat == lats - 1
    east, west = lax.rem(lon + 1, lons), lax.rem(lon + lons - 1, lons)
    facing, beside = lons - 1 - lon, lax.rem(lons - lon, lons)
    other = beside != lon
    parts = 4 if tiles % 4 == 0 else 1
    part_rows = rows // parts

    barrier = pltpu.get_barrier_semaphore()

    def greet(target_lat, target_lon):
        pl.semaphore_signal(barrier, inc=1, device_id={"lat": target_lat, "lon": target_lon}, device_id_type=MESH)

    greet(lat, east)
    greet(lat, west)

    @pl.when(jnp.logical_not(at_south))
    def _():
        greet(lat - 1, lon)

    @pl.when(jnp.logical_not(at_north))
    def _():
        greet(lat + 1, lon)

    @pl.when(at_north)
    def _():
        greet(lat, facing)

    @pl.when(jnp.logical_and(at_north, other))
    def _():
        greet(lat, beside)

    def load(source, target, index):
        copy = pltpu.make_async_copy(source, target, load_sem.at[index])
        copy.start()
        return copy

    first_loads = [load(floor_hbm, floor.at[pl.ds(0, rows)], 0)]
    part_loads = [None] * parts
    for p in (parts - 1, *range(parts - 1)):
        chunk = pl.ds(p * part_rows, part_rows)
        part_loads[p] = [
            load(ref.at[:, chunk], raw.at[i, :, chunk], 4 + 4 * p + i)
            for i, ref in enumerate((temp_hbm, salt_hbm, east_hbm, tilt_east_hbm))
        ]

    def send(source, target, index, target_lat, target_lon, receive):
        return pltpu.make_async_remote_copy(
            src_ref=source,
            dst_ref=target,
            send_sem=send_sem.at[index],
            recv_sem=recv_sem.at[receive],
            device_id={"lat": target_lat, "lon": target_lon},
            device_id_type=MESH,
        )

    rows_only = north_message.at[pl.ds(0, south_message.shape[0])]
    to_east = send(east_message, from_west, 0, lat, east, 0)
    to_west = send(west_message, from_east, 1, lat, west, 1)
    to_north = send(north_message, from_south, 2, lat + 1, lon, 2)
    to_south = send(south_message, from_north, 3, lat - 1, lon, 3)
    to_facing = send(rows_only, from_north, 4, lat, facing, 3)
    to_beside = send(beside_message, from_beside, 5, lat, beside, 4)

    lane = lax.broadcasted_iota(jnp.int32, (8, 128), 1)
    sub = lax.broadcasted_iota(jnp.int32, (8, 128), 0)
    lane_place, lane_level = lane & 3, lane >> 2
    level_f = lane_level.astype(f32)
    sub_place = sub & 3
    floor_lanes = (lane >> 1) == 52
    zero = jnp.zeros((8, 128), f32)

    def column(values, index):
        return jnp.broadcast_to(values[:, index : index + 1], (8, 128))

    def of_four(a, b, c, d):
        return jnp.where(lane_place < 2, jnp.where(lane_place == 0, a, b), jnp.where(lane_place == 2, c, d))

    def of_rows(a, b, c, d):
        return jnp.where(sub_place < 2, jnp.where(sub_place == 0, a, b), jnp.where(sub_place == 2, c, d))

    def prepare(at):
        here, padded = pl.ds(at, 8), pl.ds(at + OFF, 8)
        depth = floor[here]
        packs = [zero, zero, zero, zero]
        before, now = [None, None], [None, None]
        for k in range(levels + 1):
            if k < levels:
                wet = depth > k
                taken = lane_level == k
                values = [jnp.where(wet, raw[q, k, here], 0.0) for q in range(2)]
                values += [raw[q, k, here] for q in (2, 3)]
                for q in range(4):
                    packs[q] = jnp.where(taken, along_lanes(values[q], 4 * k + 2), packs[q])
                for q in range(2):
                    cells[q, k, padded] = values[q]
            for q in range(2):
                if k > 0:
                    below = jnp.where(wet, values[q], now[q]) if k < levels else now[q]
                    vertical[q, k - 1, padded] = (before[q] if k > 1 else now[q]) - below
                before[q], now[q] = now[q], values[q]
        depth_f = depth.astype(f32)
        own_floor = of_four(column(depth_f, 126), column(depth_f, 127), column(depth_f, 0), column(depth_f, 1))
        for q in range(4):
            packed[q, here] = packs[q]
        packed[4, here] = own_floor
        high = lane_place >= 2
        east_message[0, here] = jnp.where(high, along_lanes(packs[0], 2), packs[1])
        speeds = jnp.where(lane_place == 3, along_lanes(packs[2], 2), along_lanes(packs[3], 1))
        east_message[1, here] = jnp.where(high, speeds, own_floor)
        tracers = jnp.where(high, packs[1], along_lanes(packs[0], -2))
        west_message[here] = jnp.where(floor_lanes, along_lanes(depth_f, 104), tracers)
        floor_east[here] = jnp.where(lane == 127, 0, jnp.minimum(depth, along_lanes(depth, -1)))

    for copy in first_loads:
        copy.wait()
    last = levels // 2

    def pack_north():
        north_message[last] = zero
        for k in range(levels):
            for q in range(2):
                target = pl.ds(4 * q + 2 - 2 * (k % 2), 2)
                north_message[k // 2, target] = cells[q, k, pl.ds(OFF + rows - 2, 2)]
        north_message[last, pl.ds(0, 2)] = floor[pl.ds(rows - 2, 2)].astype(f32)

        @pl.when(at_north)
        def _():
            pack = zero
            for m in range(last + 1):
                pack = jnp.where((lane >> 1) == m, along_lanes(north_message[m], 2 * m), pack)
            beside_message[...] = pack

    order = [parts - 1, *range(parts - 1)]
    for p in order:
        for copy in part_loads[p]:
            copy.wait()
        if p == order[max(parts - 2, 0)]:
            north_loads = [load(north_hbm, raw.at[4], 20), load(tilt_north_hbm, raw.at[5], 21)]
            last_loads = [load(mix_hbm, mix, 22), load(partner_hbm, partner, 23)]

        for t in range(part_rows // 8):
            prepare(p * part_rows + 8 * t)
        if p == parts - 1:
            pack_north()

    place = lax.rem(lon, lons // 2)
    patient = jnp.logical_or(place == 0, jnp.logical_and(at_north, place == 1))
    between = jnp.logical_and(at_north, jnp.logical_or(place == 2, place == 3))
    prompt = jnp.logical_not(jnp.logical_or(patient, between))

    def meet():
        pl.semaphore_wait(barrier, jnp.where(at_south, 3, jnp.where(jnp.logical_and(at_north, other), 5, 4)))

    def send_columns(when):
        @pl.when(when)
        def _():
            to_east.start()
            to_west.start()

    def send_fold(when):
        @pl.when(jnp.logical_and(at_north, when))
        def _():
            to_facing.start()

        @pl.when(jnp.logical_and(jnp.logical_and(at_north, other), when))
        def _():
            to_beside.start()

    def send_rows(when):
        @pl.when(jnp.logical_and(jnp.logical_not(at_south), when))
        def _():
            to_south.start()

        @pl.when(jnp.logical_and(jnp.logical_not(at_north), when))
        def _():
            to_north.start()

    pl.when(prompt)(meet)
    send_columns(prompt)
    send_fold(prompt)

    for copy in north_loads:
        copy.wait()
    south_message[last] = zero
    north_message[north_message.shape[0] - 1] = zero
    for k in range(levels):
        for q in range(2):
            south_message[k // 2, pl.ds(4 * q + 2 * (k % 2), 2)] = cells[q, k, pl.ds(OFF, 2)]
            north_message[last + 1 + k // 4, pl.ds(2 * (k % 4) + q, 1)] = raw[4 + q, k, pl.ds(rows - 1, 1)]
    south_message[last, pl.ds(2, 2)] = floor[pl.ds(0, 2)].astype(f32)

    for t in range(tiles):
        both = jnp.minimum(floor[pl.ds(8 * t, 8)], floor[pl.ds(8 * t + 1, 8)])
        floor_north[pl.ds(8 * t, 8)] = both if t < tiles - 1 else jnp.where(sub == 7, 0, both)

    for copy in last_loads:
        copy.wait()

    for q in range(2):
        flux_north[q, pl.ds(0, OFF)] = zero

    def shift(k):
        for t in range(tiles):
            here, padded = pl.ds(8 * t, 8), pl.ds(OFF + 8 * t, 8)
            for q in range(2):
                slant = vertical[q, k, padded]
                moved[q, k, here] = along_lanes(cells[q, k, padded], -1)
                slants[q, k, here] = slant + along_lanes(slant, -1)

    def east_faces(k):
        for t in range(tiles):
            here, padded = pl.ds(8 * t, 8), pl.ds(OFF + 8 * t, 8)
            opened, speed = floor_east[here] > k, raw[2, k, here]
            weight, half, forth = jnp.abs(speed) * (1.0 / 6.0), 0.5 * speed, speed > 0
            spread, tilt = weight + isopycnal_rate, (0.25 * isopycnal_rate) * raw[3, k, here]
            for q in range(2):
                centre, ahead = cells[q, k, padded], moved[q, k, here]
                rise = jnp.where(lane == 127, 0.0, ahead - centre)
                flux = half * (centre + ahead) - spread * rise
                flux = flux + weight * jnp.where(forth, along_lanes(rise, 1), along_lanes(rise, -1))
                flux = flux - tilt * slants[q, k, here]
                flux_east[q, k, here] = jnp.where(opened, flux, 0.0)

    def eliminate(k, state):
        for t in range(tiles):
            here = pl.ds(8 * t, 8)
            depth = floor[here]
            opened, speed = floor_north[here] > k, raw[4, k, here]
            weight, half, forth = jnp.abs(speed) * (1.0 / 6.0), 0.5 * speed, speed > 0
            spread, tilt = weight + isopycnal_rate, (0.25 * isopycnal_rate) * raw[5, k, here]
            above, above_factor, *values = state[t]
            below = jnp.where(depth > k + 1, mix[jnp.minimum(k, levels - 2), here], 0.0)
            inverse = 1.0 / (1.0 + above + below - above * above_factor)
            factor = below * inverse
            pivot[k, here] = inverse
            rate[k, here] = below
            upper[k, here] = factor
            for q in range(2):
                row = OFF + 8 * t
                centre = cells[q, k, pl.ds(row, 8)]
                ahead, beyond = cells[q, k, pl.ds(row + 1, 8)], cells[q, k, pl.ds(row + 2, 8)]
                rise, rise_behind, rise_ahead = ahead - centre, centre - cells[q, k, pl.ds(row - 1, 8)], beyond - ahead
                if t == 0:
                    rise_behind = jnp.where(sub == 0, 0.0, rise_behind)
                if t == tiles - 1:
                    rise_ahead = jnp.where(sub >= 6, 0.0, rise_ahead)
                flux = half * (centre + ahead) - spread * rise
                flux = flux + weight * jnp.where(forth, rise_behind, rise_ahead)
                flux = flux - tilt * (vertical[q, k, pl.ds(row, 8)] + vertical[q, k, pl.ds(row + 1, 8)])
                flux = jnp.where(opened, flux, 0.0)
                flux_north[q, pl.ds(row, 8)] = flux
                interim = centre - flux + flux_north[q, pl.ds(row - 1, 8)]
                flux = flux_east[q, k, here]
                interim = interim - flux + along_lanes(flux, 1)
                values[q] = (interim + above * values[q]) * inverse
                sweep[q, k, here] = values[q]
            state[t] = (below, factor, *values)

    shift(0)
    shift(min(1, levels - 1))
    east_faces(0)

    def one_level(k, state):
        state = list(state)
        eliminate(k, state)
        east_faces(jnp.minimum(k + 1, levels - 1))
        shift(jnp.minimum(k + 2, levels - 1))
        return tuple(state)

    early, late = 6, 10
    state = lax.fori_loop(0, early, one_level, ((zero,) * 4,) * tiles)
    pl.when(between)(meet)
    send_columns(between)
    send_fold(between)
    send_rows(jnp.logical_not(patient))
    state = lax.fori_loop(early, late, one_level, state)
    pl.when(patient)(meet)
    send_rows(patient)
    send_columns(patient)
    send_fold(patient)
    lax.fori_loop(late, levels, one_level, state)

    for t in range(tiles):
        here = pl.ds(8 * t, 8)
        depth = floor[here]
        values = [zero, zero]
        for k in reversed(range(levels)):
            factor, wet = upper[k, here], depth > k
            for q in range(2):
                values[q] = sweep[q, k, here] + factor * values[q]
                solved[q, k, here] = jnp.where(wet, values[q], 0.0)

    for t in range(tiles):
        here = pl.ds(8 * t, 8)
        inverse, below = zero, zero
        for k in range(levels):
            taken = lane_level == k
            inverse = jnp.where(taken, along_lanes(pivot[k, here], 4 * k + 2), inverse)
            below = jnp.where(taken, along_lanes(rate[k, here], 4 * k + 2), below)
        packed[5, here] = inverse
        packed[6, here] = below
    for t in range(tiles):
        here = pl.ds(8 * t, 8)
        inverse, below = packed[5, here], packed[6, here]
        factors = (jnp.where(lane_level == 0, 0.0, along_lanes(below, 4)) * inverse, below * inverse)
        for i, (one, side) in enumerate(zip(factors, (4, -4))):
            two = one * along_lanes(one, side)
            four = two * along_lanes(two, 2 * side)
            five = one * along_lanes(four, side)
            ten = five * along_lanes(five, 5 * side)
            products = (one, two, one * along_lanes(two, side), four)
            products += (five, ten, five * along_lanes(ten, 5 * side), ten * along_lanes(ten, 10 * side))
            for j, product in enumerate(products):
                scan[i, j, here] = product

    for k in range(levels):
        for i, ref in enumerate((pivot, rate, upper)):
            source = max(k - 1, 0) if i == 1 else k
            row_factors[i, k] = of_rows(*(row_of(ref, source, r) for r in (rows - 2, rows - 1, 0, 1)))

    def fix_the_columns():
        to_east.wait_recv()
        to_west.wait_recv()

        def lane_vertical(values, here, depth, shift):
            above = jnp.where(lane_level == 0, here, along_lanes(values, shift + 4))
            return above - jnp.where(level_f + 1.0 < depth, along_lanes(values, shift - 4), here)

        high = lane_place >= 2
        for t in range(tiles):
            here = pl.ds(8 * t, 8)
            tracers_west, speeds_west, tracers_east = from_west[0, here], from_west[1, here], from_east[here]
            own_floor = packed[4, here]
            floor_beyond = jnp.where(lane_place == 0, column(tracers_east, 104), column(tracers_east, 105))
            far_floor = jnp.where(high, along_lanes(speeds_west, 2), floor_beyond)
            near_floor, beyond_floor = jnp.where(high, far_floor, own_floor), jnp.where(high, own_floor, far_floor)
            ahead_floor = along_lanes(beyond_floor, 1)
            speed = jnp.where(lane_place == 3, speeds_west, packed[2, here])
            slope = jnp.where(lane_place == 3, along_lanes(speeds_west, 1), packed[3, here])
            far = (
                jnp.where(high, tracers_west, tracers_east),
                jnp.where(high, along_lanes(tracers_west, 2), along_lanes(tracers_east, -2)),
            )
            for q in range(2):
                own = packed[q, here]
                near, beyond = jnp.where(high, far[q], own), jnp.where(high, own, far[q])
                ahead = along_lanes(beyond, 1)
                terms = edge_terms(
                    lane_place,
                    along_lanes,
                    level_f,
                    near,
                    beyond,
                    ahead,
                    near_floor,
                    beyond_floor,
                    ahead_floor,
                    lane_vertical(near, near, near_floor, 0),
                    lane_vertical(beyond, ahead, ahead_floor, 1),
                    speed,
                    slope,
                )
                value = terms * packed[5, here]
                for i, side in enumerate((1, -1)):
                    for base in (1, 5):
                        terms = [
                            scan[i, (4 if base == 5 else 0) + j - 1, here] * along_lanes(value, side * 4 * base * j)
                            for j in range(1, 5)
                        ]
                        value = (value + terms[0]) + (terms[1] + (terms[2] + terms[3]))
                fix_columns[q, here] = jnp.where(level_f < own_floor, value, 0.0)

    rows_first = jnp.logical_and(place == 0, jnp.logical_not(at_north))
    pl.when(jnp.logical_not(rows_first))(fix_the_columns)

    @pl.when(at_south)
    def _():
        from_south[...] = jnp.zeros(from_south.shape, f32)

    @pl.when(jnp.logical_not(at_south))
    def _():
        to_north.wait_recv()

    @pl.when(jnp.logical_not(at_north))
    def _():
        to_south.wait_recv()

    @pl.when(at_north)
    def _():
        to_facing.wait_recv()

    @pl.when(jnp.logical_and(at_north, other))
    def _():
        to_beside.wait_recv()

    @pl.when(jnp.logical_and(at_north, jnp.logical_not(other)))
    def _():
        from_beside[...] = beside_message[...]

    @pl.when(at_north)
    def _():
        index = (row_of(partner, lon) - 128 * facing + 128 * lons) & (128 * lons - 1)
        inside = index < 128
        index = index & 127
        extra = from_beside[...]
        for m in range(last + 1):
            facing_rows = jnp.take_along_axis(from_north[m], index, axis=1, mode="promise_in_bounds")
            beside_rows = jnp.take_along_axis(extra, (index + 2 * m) & 127, axis=1, mode="promise_in_bounds")
            found = jnp.where(inside, facing_rows, beside_rows)
            from_north[m] = jnp.where(
                sub_place < 2,
                jnp.where(sub_place == 0, along_rows(found, -3), along_rows(found, -1)),
                jnp.where(sub_place == 2, along_rows(found, 1), along_rows(found, 3)),
            )

    own_floor = of_rows(*(row_of(floor, r) for r in (rows - 2, rows - 1, 0, 1))).astype(f32)
    far_floor = of_rows(
        row_of(from_north, last, 2), row_of(from_north, last, 3), row_of(from_south, last, 0), row_of(from_south, last, 1)
    )
    high = sub_place >= 2

    def own_rows(k):
        lo = jnp.where(sub < 2, cells[0, k, pl.ds(OFF + rows - 2, 8)], cells[0, k, pl.ds(OFF - 2, 8)])
        hi = jnp.where(sub < 6, cells[1, k, pl.ds(OFF + rows - 6, 8)], cells[1, k, pl.ds(OFF - 6, 8)])
        return jnp.where(sub < 4, lo, hi)

    def far_rows(k):
        south, north = from_south[k // 2], from_north[k // 2]
        if k % 2 == 1:
            south, north = along_rows(south, 2), along_rows(north, -2)
        return jnp.where(high, south, north)

    near_floor, beyond_floor = jnp.where(high, far_floor, own_floor), jnp.where(high, own_floor, far_floor)
    ahead_floor = along_rows(beyond_floor, 1)
    near, beyond, ahead = [], [], []

    def row_vertical(values, depth, k):
        above = values[max(k - 1, 0)]
        below = jnp.where(depth > k + 1.0, values[k + 1], values[k]) if k + 1 < levels else values[k]
        return above - below

    value = zero
    for k in range(levels):
        while len(near) < min(k + 2, levels):
            own, far = own_rows(len(near)), far_rows(len(near))
            near.append(jnp.where(high, far, own))
            beyond.append(jnp.where(high, own, far))
            ahead.append(along_rows(beyond[-1], 1))
        speed = of_rows(
            row_of(raw, 4, k, rows - 2),
            row_of(raw, 4, k, rows - 1),
            row_of(raw, 4, k, 0),
            row_of(from_south, last + 1 + k // 4, 2 * (k % 4)),
        )
        slope = jnp.where(high, row_of(from_south, last + 1 + k // 4, 2 * (k % 4) + 1), row_of(raw, 5, k, rows - 1))
        terms = edge_terms(
            sub_place,
            along_rows,
            float(k),
            near[k],
            beyond[k],
            ahead[k],
            near_floor,
            beyond_floor,
            ahead_floor,
            row_vertical(near, near_floor, k),
            row_vertical(ahead, ahead_floor, k),
            speed,
            slope,
        )
        value = (terms + row_factors[1, k] * value if k > 0 else terms) * row_factors[0, k]
        fix_rows[k] = value
    value = zero
    for k in reversed(range(levels)):
        value = fix_rows[k] + row_factors[2, k] * value
        fix_rows[k] = jnp.where(own_floor > k, value, 0.0)

    pl.when(rows_first)(fix_the_columns)

    to_east.wait_send()
    to_west.wait_send()

    @pl.when(jnp.logical_not(at_south))
    def _():
        to_south.wait_send()

    @pl.when(jnp.logical_not(at_north))
    def _():
        to_north.wait_send()

    @pl.when(at_north)
    def _():
        to_facing.wait_send()

    @pl.when(jnp.logical_and(at_north, other))
    def _():
        to_beside.wait_send()


def finish_kernel(solved, fix_columns, fix_rows, temp_out, salt_out, result, store_sem):
    levels, rows = solved.shape[1:3]
    tiles = rows // 8
    lane = lax.broadcasted_iota(jnp.int32, (8, 128), 1)
    sub = lax.broadcasted_iota(jnp.int32, (8, 128), 0)
    edge = ((lane + 2) & 127) < 4
    outputs = (temp_out, salt_out)

    def store(t, q):
        here = pl.ds(8 * t, 8)
        return pltpu.make_async_copy(result.at[q, :, here], outputs[q].at[:, here], store_sem.at[q, t])

    def columns(t):
        here = pl.ds(8 * t, 8)
        for q in range(2):
            terms = fix_columns[q, here]
            for k in range(levels):
                result[q, k, here] = solved[q, k, here] + jnp.where(edge, along_lanes(terms, 126 - 4 * k), 0.0)

    def corners(t, wanted):
        here = pl.ds(8 * t, 8)
        for q in range(2):
            for k in range(levels):
                terms = along_rows(fix_rows[k], 2 if q else -2)
                result[q, k, here] = result[q, k, here] + jnp.where(wanted, terms, 0.0)

    for t in range(tiles):
        columns(t)
        if t == 0 or t == tiles - 1:
            corners(t, sub < 2 if t == 0 else sub >= 6)
        for q in range(2):
            store(t, q).start()

    for t in range(tiles):
        for q in range(2):
            store(t, q).wait()


def local(axes, *arguments):
    levels, rows, columns = arguments[0].shape
    partner = arguments[8].reshape(-1, columns)
    shape = (levels, rows, columns)
    padded = (2, levels, rows + 2 * OFF, columns)
    pairs = levels // 2 + 1
    north_tiles = pairs + (levels + 3) // 4
    placed = pl.BlockSpec(memory_space=pltpu.VMEM)
    solved, fix_columns, fix_rows = pl.pallas_call(
        functools.partial(step_kernel, axes),
        out_shape=(
            jax.ShapeDtypeStruct((2, *shape), f32),
            jax.ShapeDtypeStruct((2, rows, columns), f32),
            jax.ShapeDtypeStruct((levels, 8, columns), f32),
        ),
        in_specs=[pl.BlockSpec(memory_space=pl.ANY)] * 9,
        out_specs=[placed] * 3,
        scratch_shapes=[
            pltpu.VMEM((6, *shape), f32),
            pltpu.VMEM((levels - 1, rows, columns), f32),
            pltpu.VMEM((rows + OFF, columns), jnp.int32),
            pltpu.VMEM(partner.shape, jnp.int32),
            pltpu.VMEM(padded, f32),
            pltpu.VMEM(padded, f32),
            pltpu.VMEM((2, *shape), f32),
            pltpu.VMEM((2, *shape), f32),
            pltpu.VMEM((2, *shape), f32),
            pltpu.VMEM((2, rows + OFF, columns), f32),
            pltpu.VMEM((2, *shape), f32),
            pltpu.VMEM(shape, f32),
            pltpu.VMEM(shape, f32),
            pltpu.VMEM(shape, f32),
            pltpu.VMEM((rows, columns), jnp.int32),
            pltpu.VMEM((rows, columns), jnp.int32),
            pltpu.VMEM((7, rows, columns), f32),
            pltpu.VMEM((2, 8, rows, columns), f32),
            pltpu.VMEM((3, levels, 8, columns), f32),
            pltpu.VMEM((2, rows, columns), f32),
            pltpu.VMEM((rows, columns), f32),
            pltpu.VMEM((north_tiles, 8, columns), f32),
            pltpu.VMEM((pairs, 8, columns), f32),
            pltpu.VMEM((8, columns), f32),
            pltpu.VMEM((2, rows, columns), f32),
            pltpu.VMEM((rows, columns), f32),
            pltpu.VMEM((north_tiles, 8, columns), f32),
            pltpu.VMEM((pairs, 8, columns), f32),
            pltpu.VMEM((8, columns), f32),
            pltpu.SemaphoreType.DMA((24,)),
            pltpu.SemaphoreType.DMA((6,)),
            pltpu.SemaphoreType.DMA((5,)),
        ],
        compiler_params=pltpu.CompilerParams(
            collective_id=0, has_side_effects=True, vmem_limit_bytes=40 * 2**20
        ),
        name="tracer_step",
    )(*[pltpu.with_memory_space_constraint(a, pltpu.HBM) for a in (*arguments[:8], partner)])
    return pl.pallas_call(
        finish_kernel,
        out_shape=(jax.ShapeDtypeStruct(shape, f32),) * 2,
        in_specs=[placed] * 3,
        out_specs=[pl.BlockSpec(memory_space=pl.ANY)] * 2,
        scratch_shapes=[
            pltpu.VMEM((2, *shape), f32),
            pltpu.SemaphoreType.DMA((2, rows // 8)),
        ],
        compiler_params=pltpu.CompilerParams(vmem_limit_bytes=16 * 2**20),
        name="tracer_finish",
    )(solved, fix_columns, fix_rows)


def solution(mesh):
    axes = (mesh.shape["lat"], mesh.shape["lon"])
    block = P(None, "lat", "lon")
    return jax.shard_map(
        functools.partial(local, axes),
        mesh=mesh,
        in_specs=(block,) * 7 + (P("lat", "lon"), P()),
        out_specs=(block, block),
        check_vma=False,
    )
```

```python
import functools

import jax
import jax.numpy as jnp
from jax import lax
from jax.experimental import pallas as pl
from jax.experimental.pallas import tpu as pltpu
from jax.sharding import PartitionSpec as P

isopycnal_rate = 0.1
MESH = pl.DeviceIdType.MESH
f32 = jnp.float32
OFF = 8


def along_lanes(x, shift):
    return pltpu.roll(x, shift % 128, 1)


def along_rows(x, shift):
    return pltpu.roll(x, shift % 8, 0)


def row_of(ref, *index):
    *lead, row = index
    return jnp.broadcast_to(ref[(*lead, pl.ds(row, 1), slice(None))], (8, 128))


def edge_terms(
    place, turn, level, near, beyond, ahead, near_floor, beyond_floor, ahead_floor, near_vertical, ahead_vertical, speed, slope
):
    high = place >= 2
    own_floor = jnp.where(high, beyond_floor, near_floor)
    weight = jnp.abs(speed) * (1.0 / 6.0)
    full = 0.5 * speed * (near + ahead) - (weight + isopycnal_rate) * (ahead - near)
    full = full + weight * jnp.where(speed > 0, near - turn(near, 1), beyond - ahead)
    full = full - (0.25 * isopycnal_rate) * slope * (near_vertical + ahead_vertical)
    full = jnp.where(level < jnp.minimum(near_floor, ahead_floor), full, 0.0)
    part = weight * (beyond - turn(near, -1))
    part = jnp.where(jnp.where(high, speed, -speed) > 0, part, 0.0)
    part = jnp.where(level < jnp.minimum(own_floor, turn(own_floor, -1)), part, 0.0)
    flux = jnp.where((place & 1) == 1, full, part)
    at_west = jnp.where(place == 2, turn(flux, -1), jnp.where(place == 0, 0.0, turn(flux, 1)))
    return at_west - jnp.where(place == 3, 0.0, flux)


def step_kernel(
    axes,
    temp_hbm,
    salt_hbm,
    east_hbm,
    north_hbm,
    tilt_east_hbm,
    tilt_north_hbm,
    mix_hbm,
    floor_hbm,
    partner_hbm,
    solved,
    fix_columns,
    fix_rows,
    raw,
    mix,
    floor,
    partner,
    cells,
    vertical,
    moved,
    slants,
    flux_east,
    flux_north,
    sweep,
    pivot,
    rate,
    upper,
    floor_east,
    floor_north,
    packed,
    scan,
    row_factors,
    east_message,
    west_message,
    north_message,
    south_message,
    beside_message,
    from_west,
    from_east,
    from_south,
    from_north,
    from_beside,
    load_sem,
    send_sem,
    recv_sem,
):
    lats, lons = axes
    levels, rows = mix.shape[0] + 1, mix.shape[1]
    tiles = rows // 8
    lat, lon = lax.axis_index("lat"), lax.axis_index("lon")
    at_south, at_north = lat == 0, lat == lats - 1
    east, west = lax.rem(lon + 1, lons), lax.rem(lon + lons - 1, lons)
    facing, beside = lons - 1 - lon, lax.rem(lons - lon, lons)
    other = beside != lon
    parts = 4 if tiles % 4 == 0 else 1
    part_rows = rows // parts

    barrier = pltpu.get_barrier_semaphore()

    def greet(target_lat, target_lon):
        pl.semaphore_signal(barrier, inc=1, device_id={"lat": target_lat, "lon": target_lon}, device_id_type=MESH)

    greet(lat, east)
    greet(lat, west)

    @pl.when(jnp.logical_not(at_south))
    def _():
        greet(lat - 1, lon)

    @pl.when(jnp.logical_not(at_north))
    def _():
        greet(lat + 1, lon)

    @pl.when(at_north)
    def _():
        greet(lat, facing)

    @pl.when(jnp.logical_and(at_north, other))
    def _():
        greet(lat, beside)

    def load(source, target, index):
        copy = pltpu.make_async_copy(source, target, load_sem.at[index])
        copy.start()
        return copy

    first_loads = [load(floor_hbm, floor.at[pl.ds(0, rows)], 0)]
    part_loads = [None] * parts
    for p in (parts - 1, *range(parts - 1)):
        chunk = pl.ds(p * part_rows, part_rows)
        part_loads[p] = [
            load(ref.at[:, chunk], raw.at[i, :, chunk], 4 + 4 * p + i)
            for i, ref in enumerate((temp_hbm, salt_hbm, east_hbm, tilt_east_hbm))
        ]

    def send(source, target, index, target_lat, target_lon, receive):
        return pltpu.make_async_remote_copy(
            src_ref=source,
            dst_ref=target,
            send_sem=send_sem.at[index],
            recv_sem=recv_sem.at[receive],
            device_id={"lat": target_lat, "lon": target_lon},
            device_id_type=MESH,
        )

    rows_only = north_message.at[pl.ds(0, south_message.shape[0])]
    to_east = send(east_message, from_west, 0, lat, east, 0)
    to_west = send(west_message, from_east, 1, lat, west, 1)
    to_north = send(north_message, from_south, 2, lat + 1, lon, 2)
    to_south = send(south_message, from_north, 3, lat - 1, lon, 3)
    to_facing = send(rows_only, from_north, 4, lat, facing, 3)
    to_beside = send(beside_message, from_beside, 5, lat, beside, 4)

    lane = lax.broadcasted_iota(jnp.int32, (8, 128), 1)
    sub = lax.broadcasted_iota(jnp.int32, (8, 128), 0)
    lane_place, lane_level = lane & 3, lane >> 2
    level_f = lane_level.astype(f32)
    sub_place = sub & 3
    floor_lanes = (lane >> 1) == 52
    zero = jnp.zeros((8, 128), f32)

    def column(values, index):
        return jnp.broadcast_to(values[:, index : index + 1], (8, 128))

    def of_four(a, b, c, d):
        return jnp.where(lane_place < 2, jnp.where(lane_place == 0, a, b), jnp.where(lane_place == 2, c, d))

    def of_rows(a, b, c, d):
        return jnp.where(sub_place < 2, jnp.where(sub_place == 0, a, b), jnp.where(sub_place == 2, c, d))

    def prepare(at):
        here, padded = pl.ds(at, 8), pl.ds(at + OFF, 8)
        depth = floor[here]
        packs = [zero, zero, zero, zero]
        before, now = [None, None], [None, None]
        for k in range(levels + 1):
            if k < levels:
                wet = depth > k
                taken = lane_level == k
                values = [jnp.where(wet, raw[q, k, here], 0.0) for q in range(2)]
                values += [raw[q, k, here] for q in (2, 3)]
                for q in range(4):
                    packs[q] = jnp.where(taken, along_lanes(values[q], 4 * k + 2), packs[q])
                for q in range(2):
                    cells[q, k, padded] = values[q]
            for q in range(2):
                if k > 0:
                    below = jnp.where(wet, values[q], now[q]) if k < levels else now[q]
                    vertical[q, k - 1, padded] = (before[q] if k > 1 else now[q]) - below
                before[q], now[q] = now[q], values[q]
        depth_f = depth.astype(f32)
        own_floor = of_four(column(depth_f, 126), column(depth_f, 127), column(depth_f, 0), column(depth_f, 1))
        for q in range(4):
            packed[q, here] = packs[q]
        packed[4, here] = own_floor
        high = lane_place >= 2
        east_message[0, here] = jnp.where(high, along_lanes(packs[0], 2), packs[1])
        speeds = jnp.where(lane_place == 3, along_lanes(packs[2], 2), along_lanes(packs[3], 1))
        east_message[1, here] = jnp.where(high, speeds, own_floor)
        tracers = jnp.where(high, packs[1], along_lanes(packs[0], -2))
        west_message[here] = jnp.where(floor_lanes, along_lanes(depth_f, 104), tracers)
        floor_east[here] = jnp.where(lane == 127, 0, jnp.minimum(depth, along_lanes(depth, -1)))

    for copy in first_loads:
        copy.wait()
    last = levels // 2

    def pack_north():
        north_message[last] = zero
        for k in range(levels):
            for q in range(2):
                target = pl.ds(4 * q + 2 - 2 * (k % 2), 2)
                north_message[k // 2, target] = cells[q, k, pl.ds(OFF + rows - 2, 2)]
        north_message[last, pl.ds(0, 2)] = floor[pl.ds(rows - 2, 2)].astype(f32)

        @pl.when(at_north)
        def _():
            pack = zero
            for m in range(last + 1):
                pack = jnp.where((lane >> 1) == m, along_lanes(north_message[m], 2 * m), pack)
            beside_message[...] = pack

    order = [parts - 1, *range(parts - 1)]
    for p in order:
        for copy in part_loads[p]:
            copy.wait()
        if p == order[max(parts - 2, 0)]:
            north_loads = [load(north_hbm, raw.at[4], 20), load(tilt_north_hbm, raw.at[5], 21)]
            last_loads = [load(mix_hbm, mix, 22), load(partner_hbm, partner, 23)]

        for t in range(part_rows // 8):
            prepare(p * part_rows + 8 * t)
        if p == parts - 1:
            pack_north()

    place = lax.rem(lon, lons // 2)
    patient = jnp.logical_or(place == 0, jnp.logical_and(at_north, place == 1))
    between = jnp.logical_and(at_north, jnp.logical_or(place == 2, place == 3))
    prompt = jnp.logical_not(jnp.logical_or(patient, between))

    def meet():
        pl.semaphore_wait(barrier, jnp.where(at_south, 3, jnp.where(jnp.logical_and(at_north, other), 5, 4)))

    def send_columns(when):
        @pl.when(when)
        def _():
            to_east.start()
            to_west.start()

    def send_fold(when):
        @pl.when(jnp.logical_and(at_north, when))
        def _():
            to_facing.start()

        @pl.when(jnp.logical_and(jnp.logical_and(at_north, other), when))
        def _():
            to_beside.start()

    def send_rows(when):
        @pl.when(jnp.logical_and(jnp.logical_not(at_south), when))
        def _():
            to_south.start()

        @pl.when(jnp.logical_and(jnp.logical_not(at_north), when))
        def _():
            to_north.start()

    pl.when(prompt)(meet)
    send_columns(prompt)
    send_fold(prompt)

    for copy in north_loads:
        copy.wait()
    south_message[last] = zero
    north_message[north_message.shape[0] - 1] = zero
    for k in range(levels):
        for q in range(2):
            south_message[k // 2, pl.ds(4 * q + 2 * (k % 2), 2)] = cells[q, k, pl.ds(OFF, 2)]
            north_message[last + 1 + k // 4, pl.ds(2 * (k % 4) + q, 1)] = raw[4 + q, k, pl.ds(rows - 1, 1)]
    south_message[last, pl.ds(2, 2)] = floor[pl.ds(0, 2)].astype(f32)

    for t in range(tiles):
        both = jnp.minimum(floor[pl.ds(8 * t, 8)], floor[pl.ds(8 * t + 1, 8)])
        floor_north[pl.ds(8 * t, 8)] = both if t < tiles - 1 else jnp.where(sub == 7, 0, both)

    for copy in last_loads:
        copy.wait()

    for q in range(2):
        flux_north[q, pl.ds(0, OFF)] = zero

    def shift(k):
        for t in range(tiles):
            here, padded = pl.ds(8 * t, 8), pl.ds(OFF + 8 * t, 8)
            for q in range(2):
                slant = vertical[q, k, padded]
                moved[q, k, here] = along_lanes(cells[q, k, padded], -1)
                slants[q, k, here] = slant + along_lanes(slant, -1)

    def east_faces(k):
        for t in range(tiles):
            here, padded = pl.ds(8 * t, 8), pl.ds(OFF + 8 * t, 8)
            opened, speed = floor_east[here] > k, raw[2, k, here]
            weight, half, forth = jnp.abs(speed) * (1.0 / 6.0), 0.5 * speed, speed > 0
            spread, tilt = weight + isopycnal_rate, (0.25 * isopycnal_rate) * raw[3, k, here]
            for q in range(2):
                centre, ahead = cells[q, k, padded], moved[q, k, here]
                rise = jnp.where(lane == 127, 0.0, ahead - centre)
                flux = half * (centre + ahead) - spread * rise
                flux = flux + weight * jnp.where(forth, along_lanes(rise, 1), along_lanes(rise, -1))
                flux = flux - tilt * slants[q, k, here]
                flux_east[q, k, here] = jnp.where(opened, flux, 0.0)

    def eliminate(k, state):
        for t in range(tiles):
            here = pl.ds(8 * t, 8)
            depth = floor[here]
            opened, speed = floor_north[here] > k, raw[4, k, here]
            weight, half, forth = jnp.abs(speed) * (1.0 / 6.0), 0.5 * speed, speed > 0
            spread, tilt = weight + isopycnal_rate, (0.25 * isopycnal_rate) * raw[5, k, here]
            above, above_factor, *values = state[t]
            below = jnp.where(depth > k + 1, mix[jnp.minimum(k, levels - 2), here], 0.0)
            inverse = 1.0 / (1.0 + above + below - above * above_factor)
            factor = below * inverse
            pivot[k, here] = inverse
            rate[k, here] = below
            upper[k, here] = factor
            for q in range(2):
                row = OFF + 8 * t
                centre = cells[q, k, pl.ds(row, 8)]
                ahead, beyond = cells[q, k, pl.ds(row + 1, 8)], cells[q, k, pl.ds(row + 2, 8)]
                rise, rise_behind, rise_ahead = ahead - centre, centre - cells[q, k, pl.ds(row - 1, 8)], beyond - ahead
                if t == 0:
                    rise_behind = jnp.where(sub == 0, 0.0, rise_behind)
                if t == tiles - 1:
                    rise_ahead = jnp.where(sub >= 6, 0.0, rise_ahead)
                flux = half * (centre + ahead) - spread * rise
                flux = flux + weight * jnp.where(forth, rise_behind, rise_ahead)
                flux = flux - tilt * (vertical[q, k, pl.ds(row, 8)] + vertical[q, k, pl.ds(row + 1, 8)])
                flux = jnp.where(opened, flux, 0.0)
                flux_north[q, pl.ds(row, 8)] = flux
                interim = centre - flux + flux_north[q, pl.ds(row - 1, 8)]
                flux = flux_east[q, k, here]
                interim = interim - flux + along_lanes(flux, 1)
                values[q] = (interim + above * values[q]) * inverse
                sweep[q, k, here] = values[q]
            state[t] = (below, factor, *values)

    shift(0)
    shift(min(1, levels - 1))
    east_faces(0)

    def one_level(k, state):
        state = list(state)
        eliminate(k, state)
        east_faces(jnp.minimum(k + 1, levels - 1))
        shift(jnp.minimum(k + 2, levels - 1))
        return tuple(state)

    early, late = 6, 8
    state = lax.fori_loop(0, early, one_level, ((zero,) * 4,) * tiles)
    pl.when(between)(meet)
    send_columns(between)
    send_fold(between)
    send_rows(jnp.logical_not(patient))
    state = lax.fori_loop(early, late, one_level, state)
    pl.when(patient)(meet)
    west_first = jnp.logical_and(patient, jnp.logical_or(jnp.logical_not(at_north), lon == lons // 2))
    pl.when(west_first)(to_west.start)
    send_rows(patient)
    pl.when(jnp.logical_and(patient, jnp.logical_not(west_first)))(to_west.start)
    pl.when(patient)(to_east.start)
    send_fold(patient)
    lax.fori_loop(late, levels, one_level, state)

    for t in range(tiles):
        here = pl.ds(8 * t, 8)
        depth = floor[here]
        values = [zero, zero]
        for k in reversed(range(levels)):
            factor, wet = upper[k, here], depth > k
            for q in range(2):
                values[q] = sweep[q, k, here] + factor * values[q]
                solved[q, k, here] = jnp.where(wet, values[q], 0.0)

    for t in range(tiles):
        here = pl.ds(8 * t, 8)
        inverse, below = zero, zero
        for k in range(levels):
            taken = lane_level == k
            inverse = jnp.where(taken, along_lanes(pivot[k, here], 4 * k + 2), inverse)
            below = jnp.where(taken, along_lanes(rate[k, here], 4 * k + 2), below)
        packed[5, here] = inverse
        packed[6, here] = below
    for t in range(tiles):
        here = pl.ds(8 * t, 8)
        inverse, below = packed[5, here], packed[6, here]
        factors = (jnp.where(lane_level == 0, 0.0, along_lanes(below, 4)) * inverse, below * inverse)
        for i, (one, side) in enumerate(zip(factors, (4, -4))):
            two = one * along_lanes(one, side)
            four = two * along_lanes(two, 2 * side)
            five = one * along_lanes(four, side)
            ten = five * along_lanes(five, 5 * side)
            products = (one, two, one * along_lanes(two, side), four)
            products += (five, ten, five * along_lanes(ten, 5 * side), ten * along_lanes(ten, 10 * side))
            for j, product in enumerate(products):
                scan[i, j, here] = product

    for k in range(levels):
        for i, ref in enumerate((pivot, rate, upper)):
            source = max(k - 1, 0) if i == 1 else k
            row_factors[i, k] = of_rows(*(row_of(ref, source, r) for r in (rows - 2, rows - 1, 0, 1)))

    def fix_the_columns():
        to_east.wait_recv()
        to_west.wait_recv()

        def lane_vertical(values, here, depth, shift):
            above = jnp.where(lane_level == 0, here, along_lanes(values, shift + 4))
            return above - jnp.where(level_f + 1.0 < depth, along_lanes(values, shift - 4), here)

        high = lane_place >= 2
        for t in range(tiles):
            here = pl.ds(8 * t, 8)
            tracers_west, speeds_west, tracers_east = from_west[0, here], from_west[1, here], from_east[here]
            own_floor = packed[4, here]
            floor_beyond = jnp.where(lane_place == 0, column(tracers_east, 104), column(tracers_east, 105))
            far_floor = jnp.where(high, along_lanes(speeds_west, 2), floor_beyond)
            near_floor, beyond_floor = jnp.where(high, far_floor, own_floor), jnp.where(high, own_floor, far_floor)
            ahead_floor = along_lanes(beyond_floor, 1)
            speed = jnp.where(lane_place == 3, speeds_west, packed[2, here])
            slope = jnp.where(lane_place == 3, along_lanes(speeds_west, 1), packed[3, here])
            far = (
                jnp.where(high, tracers_west, tracers_east),
                jnp.where(high, along_lanes(tracers_west, 2), along_lanes(tracers_east, -2)),
            )
            for q in range(2):
                own = packed[q, here]
                near, beyond = jnp.where(high, far[q], own), jnp.where(high, own, far[q])
                ahead = along_lanes(beyond, 1)
                terms = edge_terms(
                    lane_place,
                    along_lanes,
                    level_f,
                    near,
                    beyond,
                    ahead,
                    near_floor,
                    beyond_floor,
                    ahead_floor,
                    lane_vertical(near, near, near_floor, 0),
                    lane_vertical(beyond, ahead, ahead_floor, 1),
                    speed,
                    slope,
                )
                value = terms * packed[5, here]
                for i, side in enumerate((1, -1)):
                    for base in (1, 5):
                        terms = [
                            scan[i, (4 if base == 5 else 0) + j - 1, here] * along_lanes(value, side * 4 * base * j)
                            for j in range(1, 5)
                        ]
                        value = (value + terms[0]) + (terms[1] + (terms[2] + terms[3]))
                fix_columns[q, here] = jnp.where(level_f < own_floor, value, 0.0)

    rows_first = jnp.logical_and(place == 0, jnp.logical_not(at_north))
    pl.when(jnp.logical_not(rows_first))(fix_the_columns)

    @pl.when(at_south)
    def _():
        from_south[...] = jnp.zeros(from_south.shape, f32)

    @pl.when(jnp.logical_not(at_south))
    def _():
        to_north.wait_recv()

    @pl.when(jnp.logical_not(at_north))
    def _():
        to_south.wait_recv()

    @pl.when(at_north)
    def _():
        to_facing.wait_recv()

    @pl.when(jnp.logical_and(at_north, other))
    def _():
        to_beside.wait_recv()

    @pl.when(jnp.logical_and(at_north, jnp.logical_not(other)))
    def _():
        from_beside[...] = beside_message[...]

    @pl.when(at_north)
    def _():
        index = (row_of(partner, lon) - 128 * facing + 128 * lons) & (128 * lons - 1)
        inside = index < 128
        index = index & 127
        extra = from_beside[...]
        for m in range(last + 1):
            facing_rows = jnp.take_along_axis(from_north[m], index, axis=1, mode="promise_in_bounds")
            beside_rows = jnp.take_along_axis(extra, (index + 2 * m) & 127, axis=1, mode="promise_in_bounds")
            found = jnp.where(inside, facing_rows, beside_rows)
            from_north[m] = jnp.where(
                sub_place < 2,
                jnp.where(sub_place == 0, along_rows(found, -3), along_rows(found, -1)),
                jnp.where(sub_place == 2, along_rows(found, 1), along_rows(found, 3)),
            )

    own_floor = of_rows(*(row_of(floor, r) for r in (rows - 2, rows - 1, 0, 1))).astype(f32)
    far_floor = of_rows(
        row_of(from_north, last, 2), row_of(from_north, last, 3), row_of(from_south, last, 0), row_of(from_south, last, 1)
    )
    high = sub_place >= 2

    def own_rows(k):
        lo = jnp.where(sub < 2, cells[0, k, pl.ds(OFF + rows - 2, 8)], cells[0, k, pl.ds(OFF - 2, 8)])
        hi = jnp.where(sub < 6, cells[1, k, pl.ds(OFF + rows - 6, 8)], cells[1, k, pl.ds(OFF - 6, 8)])
        return jnp.where(sub < 4, lo, hi)

    def far_rows(k):
        south, north = from_south[k // 2], from_north[k // 2]
        if k % 2 == 1:
            south, north = along_rows(south, 2), along_rows(north, -2)
        return jnp.where(high, south, north)

    near_floor, beyond_floor = jnp.where(high, far_floor, own_floor), jnp.where(high, own_floor, far_floor)
    ahead_floor = along_rows(beyond_floor, 1)
    near, beyond, ahead = [], [], []

    def row_vertical(values, depth, k):
        above = values[max(k - 1, 0)]
        below = jnp.where(depth > k + 1.0, values[k + 1], values[k]) if k + 1 < levels else values[k]
        return above - below

    value = zero
    for k in range(levels):
        while len(near) < min(k + 2, levels):
            own, far = own_rows(len(near)), far_rows(len(near))
            near.append(jnp.where(high, far, own))
            beyond.append(jnp.where(high, own, far))
            ahead.append(along_rows(beyond[-1], 1))
        speed = of_rows(
            row_of(raw, 4, k, rows - 2),
            row_of(raw, 4, k, rows - 1),
            row_of(raw, 4, k, 0),
            row_of(from_south, last + 1 + k // 4, 2 * (k % 4)),
        )
        slope = jnp.where(high, row_of(from_south, last + 1 + k // 4, 2 * (k % 4) + 1), row_of(raw, 5, k, rows - 1))
        terms = edge_terms(
            sub_place,
            along_rows,
            float(k),
            near[k],
            beyond[k],
            ahead[k],
            near_floor,
            beyond_floor,
            ahead_floor,
            row_vertical(near, near_floor, k),
            row_vertical(ahead, ahead_floor, k),
            speed,
            slope,
        )
        value = (terms + row_factors[1, k] * value if k > 0 else terms) * row_factors[0, k]
        fix_rows[k] = value
    value = zero
    for k in reversed(range(levels)):
        value = fix_rows[k] + row_factors[2, k] * value
        fix_rows[k] = jnp.where(own_floor > k, value, 0.0)

    pl.when(rows_first)(fix_the_columns)

    to_east.wait_send()
    to_west.wait_send()

    @pl.when(jnp.logical_not(at_south))
    def _():
        to_south.wait_send()

    @pl.when(jnp.logical_not(at_north))
    def _():
        to_north.wait_send()

    @pl.when(at_north)
    def _():
        to_facing.wait_send()

    @pl.when(jnp.logical_and(at_north, other))
    def _():
        to_beside.wait_send()


def finish_kernel(solved, fix_columns, fix_rows, temp_out, salt_out, result, store_sem):
    levels, rows = solved.shape[1:3]
    tiles = rows // 8
    lane = lax.broadcasted_iota(jnp.int32, (8, 128), 1)
    sub = lax.broadcasted_iota(jnp.int32, (8, 128), 0)
    edge = ((lane + 2) & 127) < 4
    outputs = (temp_out, salt_out)

    def store(t, q):
        here = pl.ds(8 * t, 8)
        return pltpu.make_async_copy(result.at[q, :, here], outputs[q].at[:, here], store_sem.at[q, t])

    def columns(t):
        here = pl.ds(8 * t, 8)
        for q in range(2):
            terms = fix_columns[q, here]
            for k in range(levels):
                result[q, k, here] = solved[q, k, here] + jnp.where(edge, along_lanes(terms, 126 - 4 * k), 0.0)

    def corners(t, wanted):
        here = pl.ds(8 * t, 8)
        for q in range(2):
            for k in range(levels):
                terms = along_rows(fix_rows[k], 2 if q else -2)
                result[q, k, here] = result[q, k, here] + jnp.where(wanted, terms, 0.0)

    for t in (*range(1, tiles // 2), 0, tiles - 1, *range(tiles // 2, tiles - 1)):
        columns(t)
        if t == 0 or t == tiles - 1:
            corners(t, sub < 2 if t == 0 else sub >= 6)
        for q in range(2):
            store(t, q).start()

    for t in range(tiles):
        for q in range(2):
            store(t, q).wait()


def local(axes, *arguments):
    levels, rows, columns = arguments[0].shape
    partner = arguments[8].reshape(-1, columns)
    shape = (levels, rows, columns)
    padded = (2, levels, rows + 2 * OFF, columns)
    pairs = levels // 2 + 1
    north_tiles = pairs + (levels + 3) // 4
    placed = pl.BlockSpec(memory_space=pltpu.VMEM)
    solved, fix_columns, fix_rows = pl.pallas_call(
        functools.partial(step_kernel, axes),
        out_shape=(
            jax.ShapeDtypeStruct((2, *shape), f32),
            jax.ShapeDtypeStruct((2, rows, columns), f32),
            jax.ShapeDtypeStruct((levels, 8, columns), f32),
        ),
        in_specs=[pl.BlockSpec(memory_space=pl.ANY)] * 9,
        out_specs=[placed] * 3,
        scratch_shapes=[
            pltpu.VMEM((6, *shape), f32),
            pltpu.VMEM((levels - 1, rows, columns), f32),
            pltpu.VMEM((rows + OFF, columns), jnp.int32),
            pltpu.VMEM(partner.shape, jnp.int32),
            pltpu.VMEM(padded, f32),
            pltpu.VMEM(padded, f32),
            pltpu.VMEM((2, *shape), f32),
            pltpu.VMEM((2, *shape), f32),
            pltpu.VMEM((2, *shape), f32),
            pltpu.VMEM((2, rows + OFF, columns), f32),
            pltpu.VMEM((2, *shape), f32),
            pltpu.VMEM(shape, f32),
            pltpu.VMEM(shape, f32),
            pltpu.VMEM(shape, f32),
            pltpu.VMEM((rows, columns), jnp.int32),
            pltpu.VMEM((rows, columns), jnp.int32),
            pltpu.VMEM((7, rows, columns), f32),
            pltpu.VMEM((2, 8, rows, columns), f32),
            pltpu.VMEM((3, levels, 8, columns), f32),
            pltpu.VMEM((2, rows, columns), f32),
            pltpu.VMEM((rows, columns), f32),
            pltpu.VMEM((north_tiles, 8, columns), f32),
            pltpu.VMEM((pairs, 8, columns), f32),
            pltpu.VMEM((8, columns), f32),
            pltpu.VMEM((2, rows, columns), f32),
            pltpu.VMEM((rows, columns), f32),
            pltpu.VMEM((north_tiles, 8, columns), f32),
            pltpu.VMEM((pairs, 8, columns), f32),
            pltpu.VMEM((8, columns), f32),
            pltpu.SemaphoreType.DMA((24,)),
            pltpu.SemaphoreType.DMA((6,)),
            pltpu.SemaphoreType.DMA((5,)),
        ],
        compiler_params=pltpu.CompilerParams(
            collective_id=0, has_side_effects=True, vmem_limit_bytes=40 * 2**20
        ),
        name="tracer_step",
    )(*[pltpu.with_memory_space_constraint(a, pltpu.HBM) for a in (*arguments[:8], partner)])
    return pl.pallas_call(
        finish_kernel,
        out_shape=(jax.ShapeDtypeStruct(shape, f32),) * 2,
        in_specs=[placed] * 3,
        out_specs=[pl.BlockSpec(memory_space=pl.ANY)] * 2,
        scratch_shapes=[
            pltpu.VMEM((2, *shape), f32),
            pltpu.SemaphoreType.DMA((2, rows // 8)),
        ],
        compiler_params=pltpu.CompilerParams(vmem_limit_bytes=16 * 2**20),
        name="tracer_finish",
    )(solved, fix_columns, fix_rows)


def solution(mesh):
    axes = (mesh.shape["lat"], mesh.shape["lon"])
    block = P(None, "lat", "lon")
    return jax.shard_map(
        functools.partial(local, axes),
        mesh=mesh,
        in_specs=(block,) * 7 + (P("lat", "lon"), P()),
        out_specs=(block, block),
        check_vma=False,
    )
```
